256 devices in a mesh: depth: 16 (over x, y_hi, core), tile: 16 (over y_lo, z).
Axes of the slice: x: 4, y: 4 (y_hi: 2, y_lo: 2; y = y_hi * 2 + y_lo), z: 8, core: 2. Of those that a mesh axis runs over, the one named last changes fastest.
Arguments:
- volume: float32 [32, 2048, 384], P('depth', 'tile'), may hold values from -6 to 6
- point_spread: float32 [32, 255, 255], P('depth'), may hold values from -0.00390625 to 0.00390625
- measured: float32 [2048, 384], P('tile'), may hold values from -6 to 6
Outputs:
- volume_next: float32 [32, 2048, 384], P('depth', 'tile')
- residual: float32 [2048, 384], P('tile')
The draws below stay inside these ranges and needn't reach their ends.
All inputs are finite; a program needn't handle non-finite values.
Results may differ from the reference program's by a relative error of at most 0.0003.
Values sent between devices are 32-bit elements; how exact they have to be, the bound alone decides.
A program may use at most 64 MiB of HBM per device.

```python
import jax
import jax.numpy as jnp
from jax import lax

K = 255
HALO = 127
DEPTHS = 32
NW = 384
NH = 2048


def block_scale(stream_key, dims, pieces, low, top_value):
    level = 1.0
    for position, shards_of in pieces:
        heights = jax.random.uniform(jax.random.fold_in(jax.random.fold_in(stream_key, 6), position), (shards_of,), jnp.float32, low / len(pieces), top_value / len(pieces))
        level = level * jnp.repeat(jnp.exp(heights), dims[position] // shards_of).reshape((-1,) + (1,) * (len(dims) - 1 - position))
    return level


def bell_draw(own_key, extent, width, reach, split=(), dtype=jnp.bfloat16):
    entries = width * jax.random.normal(own_key, extent, jnp.float32)
    if split:
        entries = entries * block_scale(own_key, extent, split, -0.22, 0.18)
    return jnp.clip(entries, -reach, reach).astype(dtype)


def setup_inputs(seed: int = 0) -> dict:
    splits = jax.random.split(jax.random.key(seed), 4)
    return {
        "volume": bell_draw(splits[0], (DEPTHS, NH, NW), 1.0, 6.0, ((0, 16), (1, 16)), jnp.float32),
        "point_spread": bell_draw(splits[1], (DEPTHS, K, K), (K * K * DEPTHS) ** -0.5, 0.00390625, ((0, 16),), jnp.float32),
        "measured": bell_draw(splits[2], (NH, NW), 1.0, 6.0, ((0, 16),), jnp.float32),
    }


step_size = 2.0
threshold = 0.5


def reference(volume, point_spread, measured):
    height_count = measured.shape[0]
    width_count = measured.shape[1]
    shape_full = (height_count + K - 1, width_count + K - 1)

    def plane_spectrum(pair):
        plane, kernel = pair
        return jnp.fft.rfft2(plane, s=shape_full) * jnp.fft.rfft2(kernel, s=shape_full)

    total = jnp.sum(lax.map(plane_spectrum, (volume, point_spread)), axis=0)
    full_image = jnp.fft.irfft2(total, s=shape_full)
    projection = full_image[HALO:HALO + height_count, HALO:HALO + width_count].astype(jnp.float32)
    residual = projection - measured
    residual_spectrum = jnp.fft.rfft2(residual, s=shape_full)

    def plane_update(pair):
        plane, kernel = pair
        flipped = kernel[::-1, ::-1]
        back_image = jnp.fft.irfft2(residual_spectrum * jnp.fft.rfft2(flipped, s=shape_full), s=shape_full)
        gradient = back_image[HALO:HALO + height_count, HALO:HALO + width_count].astype(jnp.float32)
        shifted = plane - step_size * gradient
        return jnp.sign(shifted) * jnp.maximum(jnp.abs(shifted) - threshold, 0.0)

    volume_next = lax.map(plane_update, (volume, point_spread))
    return volume_next, residual
```

```python
import functools
import math

import jax
import jax.numpy as jnp
import ml_dtypes
import numpy as np
from jax import lax
from jax.experimental import pallas as pl
from jax.experimental.pallas import tpu as pltpu
from jax.sharding import PartitionSpec as P

step_size = 2.0
threshold = 0.5
f32 = jnp.float32
bf16 = jnp.bfloat16
MESH = pl.DeviceIdType.MESH


def halves(table):
    table = table.astype(np.float32)
    high = table.astype(ml_dtypes.bfloat16)
    low = (table - high.astype(np.float32)).astype(ml_dtypes.bfloat16)
    return np.stack([high, low])


def tables(rows, width, size):
    freq_rows, freq_cols = 3 * rows, width + 128
    half = freq_cols // 2
    reach = (size - 1) // 2
    omega = math.pi * (2 * np.arange(half) + 1) / freq_cols
    across = np.arange(width)[:, None] * omega[None, :]
    col = np.concatenate([np.cos(across), -np.sin(across)], 1)
    back = col.T * (2.0 / (freq_cols * freq_rows))
    across_k = (np.arange(size + 1) - reach)[:, None] * omega[None, :]
    col_k = np.concatenate([np.cos(across_k), -np.sin(across_k)], 1)
    u = np.arange(freq_rows)
    down = 2 * math.pi / freq_rows * (u[:, None] * u[None, :] % freq_rows)
    row = np.concatenate([np.cos(down), np.sin(down)], 0)
    down_k = 2 * math.pi / freq_rows * (u[:, None] * (np.arange(size + 1) - reach)[None, :] % freq_rows)
    row_k = np.concatenate([np.cos(down_k), np.sin(down_k)], 0)
    return [halves(t) for t in (col, back, col_k, row, row_k)]


def split(x):
    high = x.astype(bf16)
    return high, (x - high.astype(f32)).astype(bf16)


def product(a, b):
    left = jnp.concatenate([a[0], a[1], a[0]], axis=1)
    right = jnp.concatenate([b[0], b[0], b[1]], axis=0)
    return jnp.dot(left, right, preferred_element_type=f32)


def turned(a, sign):
    m, n = a.shape[0] // 2, a.shape[1] // 2
    real = a[:m, :n] + sign * a[m:, n:]
    imaginary = a[:m, n:] - sign * a[m:, :n]
    return real, imaginary


def kernel(
    chips,
    strips,
    volume_ref,
    spread_ref,
    measured_ref,
    col_ref,
    back_ref,
    col_k_ref,
    row_ref,
    row_k_ref,
    next_ref,
    residual_ref,
    pad_ref,
    optic_ref,
    mid_ref,
    part_ref,
    pair_ref,
    held_ref,
    beside_ref,
    own_ref,
    piece_ref,
    mine_ref,
    final_ref,
    full_ref,
    pair_sems,
    tile_sems,
    piece_sems,
    final_sems,
    half_sems,
    halo_sems,
    relay_sems,
):
    depth, tile = lax.axis_index("depth"), lax.axis_index("tile")
    chip, core = depth // 2, depth % 2
    partner = chip * 2 + (1 - core)
    above, below = (tile + 1) % strips, (tile + strips - 1) % strips
    others = [(chip + s) % chips * 2 + core for s in range(chips)]
    planes, rows, width = volume_ref.shape
    size = spread_ref.shape[1]
    half_rows = rows // 2
    freq_rows, freq_cols = 3 * rows, width + 128
    half = freq_cols // 2

    barrier = pltpu.get_barrier_semaphore()
    peers = [(partner, tile), (depth, above), (depth, below)] + [(o, tile) for o in others[1:]]
    for d, t in peers:
        pl.semaphore_signal(barrier, inc=1, device_id=(d, t), device_id_type=MESH)

    def remote(src, dst, sems, index, d, t):
        return pltpu.make_async_remote_copy(
            src_ref=src,
            dst_ref=dst,
            send_sem=sems.at[0, index],
            recv_sem=sems.at[1, index],
            device_id=(d, t),
            device_id_type=MESH,
        )

    def pair(ref, *index):
        return ref[(0, *index)], ref[(1, *index)]

    pad_ref[...] = jnp.zeros_like(pad_ref)
    for d in range(planes):
        pad_ref[d, 0:size, 0:size] = spread_ref[d]
    stacked = pad_ref[...].reshape(planes * (size + 1), size + 1)
    optic_cols = product(split(stacked), pair(col_k_ref))
    plane_cols = product(split(volume_ref[...].reshape(planes * rows, width)), pair(col_ref))
    for d in range(planes):
        optic = split(optic_cols[d * (size + 1) : (d + 1) * (size + 1)])
        real, imaginary = turned(product(pair(row_k_ref), optic), 1.0)
        optic_ref[d, 0], optic_ref[d, 1] = real, imaginary
    for d in range(planes):
        plane = split(plane_cols[d * rows : (d + 1) * rows])
        row_part = pair(row_ref, slice(None), slice(0, rows))
        real, imaginary = turned(product(row_part, plane), 1.0)
        optic_real, optic_imaginary = optic_ref[d, 0], optic_ref[d, 1]
        sum_real = optic_real * real - optic_imaginary * imaginary
        sum_imaginary = optic_real * imaginary + optic_imaginary * real
        if d == 0:
            mid_ref[0], mid_ref[1] = sum_real, sum_imaginary
        else:
            mid_ref[0] += sum_real
            mid_ref[1] += sum_imaginary
    total = split(jnp.concatenate([mid_ref[0], mid_ref[1]], axis=1))
    real, imaginary = turned(product(pair(row_ref), total), -1.0)
    mixed = jnp.concatenate([real, imaginary], axis=1)
    part_ref[...] = product(split(mixed), pair(back_ref)).reshape(part_ref.shape)

    pl.semaphore_wait(barrier, len(peers))

    copies = []
    for b in (1, 2, 0):
        copy = remote(part_ref.at[b, 1 - core], pair_ref.at[b], pair_sems, b, partner, tile)
        copy.start()
        copies.append(copy)
    sends = list(copies)
    for b, t in ((1, above), (2, below)):
        copies[b - 1].wait_recv()
        held_ref[b - 1] = part_ref[b, core] + pair_ref[b]
        copy = remote(held_ref.at[b - 1], beside_ref.at[b - 1], tile_sems, b - 1, depth, t)
        copy.start()
        copies.append(copy)
        sends.append(copy)
    copies[2].wait_recv()
    own = part_ref[0, core] + pair_ref[0]
    copies[3].wait_recv()
    own += jnp.where(tile > 0, beside_ref[0], 0.0)
    copies[4].wait_recv()
    own += jnp.where(tile < strips - 1, beside_ref[1], 0.0)
    own_ref[...] = own.reshape(own_ref.shape)

    pieces = []
    for s in range(1, chips):
        copy = remote(own_ref.at[(chip + s) % chips], piece_ref.at[s], piece_sems, s, others[s], tile)
        copy.start()
        pieces.append(copy)
    sends += pieces
    piece = own_ref[chip]
    for s in range(1, chips):
        pieces[s - 1].wait_recv()
        piece += piece_ref[s]
    length = half_rows // chips
    start = pl.multiple_of(core * half_rows + chip * length, length)
    mine_ref[...] = piece - measured_ref[pl.ds(start, length), :]

    finals = []
    for s in range(1, chips):
        copy = remote(mine_ref, final_ref.at[chip], final_sems, s, others[s], tile)
        copy.start()
        finals.append(copy)
    sends += finals
    final_ref[chip] = mine_ref[...]
    for copy in finals:
        copy.wait_recv()
    halves_out = final_ref[...].reshape(half_rows, width)
    full_ref[0, core] = halves_out
    half_copy = remote(full_ref.at[0, core], full_ref.at[0, core], half_sems, 0, partner, tile)
    half_copy.start()
    up = remote(full_ref.at[0, core], full_ref.at[2, core], halo_sems, 0, depth, above)
    up.start()
    down = remote(full_ref.at[0, core], full_ref.at[1, core], halo_sems, 1, depth, below)
    down.start()
    up.wait_recv()
    relay_up = remote(full_ref.at[2, core], full_ref.at[2, core], relay_sems, 0, partner, tile)
    relay_up.start()
    down.wait_recv()
    relay_down = remote(full_ref.at[1, core], full_ref.at[1, core], relay_sems, 1, partner, tile)
    relay_down.start()
    half_copy.wait_recv()
    relay_up.wait_recv()
    relay_down.wait_recv()
    sends += [half_copy, up, down, relay_up, relay_down]

    strip = full_ref[0].reshape(rows, width)
    residual_ref[...] = strip
    after = jnp.where(tile < strips - 1, full_ref[1].reshape(rows, width), 0.0)
    before = jnp.where(tile > 0, full_ref[2].reshape(rows, width), 0.0)
    block = jnp.concatenate([strip, after, before], axis=0)
    block_cols = product(split(block), pair(col_ref))
    real, imaginary = turned(product(pair(row_ref), split(block_cols)), 1.0)
    mid_ref[0], mid_ref[1] = real, imaginary
    for d in range(planes):
        real, imaginary = mid_ref[0], mid_ref[1]
        optic_real, optic_imaginary = optic_ref[d, 0], optic_ref[d, 1]
        grad_real = optic_real * real + optic_imaginary * imaginary
        grad_imaginary = optic_real * imaginary - optic_imaginary * real
        grad = split(jnp.concatenate([grad_real, grad_imaginary], axis=1))
        ends = [jnp.concatenate([row_ref[p, 0:rows], row_ref[p, freq_rows : freq_rows + rows]], axis=0) for p in range(2)]
        real, imaginary = turned(product(ends, grad), -1.0)
        mixed = split(jnp.concatenate([real, imaginary], axis=1))
        gradient = product(mixed, pair(back_ref))
        shifted = volume_ref[d] - step_size * gradient
        next_ref[d] = shifted - jnp.clip(shifted, -threshold, threshold)
    for copy in sends:
        copy.wait_send()


def per_device(volume, point_spread, measured):
    planes, rows, width = volume.shape
    size = point_spread.shape[1]
    chips, strips = lax.axis_size("depth") // 2, lax.axis_size("tile")
    constants = [jnp.asarray(t) for t in tables(rows, width, size)]
    half_rows = rows // 2
    length = half_rows // chips
    freq_rows, half = 3 * rows, (width + 128) // 2
    vmem = pl.BlockSpec(memory_space=pltpu.VMEM)
    dma = pltpu.SemaphoreType.DMA
    return pl.pallas_call(
        functools.partial(kernel, chips, strips),
        out_shape=(
            jax.ShapeDtypeStruct((planes, rows, width), f32),
            jax.ShapeDtypeStruct((rows, width), f32),
        ),
        in_specs=[vmem] * 8,
        out_specs=(vmem, vmem),
        scratch_shapes=[
            pltpu.VMEM((planes, size + 1, size + 1), f32),
            pltpu.VMEM((planes, 2, freq_rows, half), f32),
            pltpu.VMEM((2, freq_rows, half), f32),
            pltpu.VMEM((3, 2, half_rows, width), f32),
            pltpu.VMEM((3, half_rows, width), f32),
            pltpu.VMEM((2, half_rows, width), f32),
            pltpu.VMEM((2, half_rows, width), f32),
            pltpu.VMEM((chips, length, width), f32),
            pltpu.VMEM((chips, length, width), f32),
            pltpu.VMEM((length, width), f32),
            pltpu.VMEM((chips, length, width), f32),
            pltpu.VMEM((3, 2, half_rows, width), f32),
            dma((2, 3)),
            dma((2, 2)),
            dma((2, chips)),
            dma((2, chips)),
            dma((2, 1)),
            dma((2, 2)),
            dma((2, 2)),
        ],
        compiler_params=pltpu.CompilerParams(
            collective_id=0, has_side_effects=True, vmem_limit_bytes=60 * 2**20
        ),
    )(volume, point_spread, measured, *constants)


def solution(mesh):
    placed = (P("depth", "tile", None), P("depth", None, None), P("tile", None))
    return jax.shard_map(
        per_device,
        mesh=mesh,
        in_specs=placed,
        out_specs=(P("depth", "tile", None), P("tile", None)),
        check_vma=False,
    )
```

```python
import functools
import math

import jax
import jax.numpy as jnp
import ml_dtypes
import numpy as np
from jax import lax
from jax.experimental import pallas as pl
from jax.experimental.pallas import tpu as pltpu
from jax.sharding import PartitionSpec as P

step_size = 2.0
threshold = 0.5
f32 = jnp.float32
bf16 = jnp.bfloat16
MESH = pl.DeviceIdType.MESH


def halves(table):
    table = table.astype(np.float32)
    high = table.astype(ml_dtypes.bfloat16)
    low = (table - high.astype(np.float32)).astype(ml_dtypes.bfloat16)
    return np.stack([high, low])


def tables(rows, width, size):
    freq_rows, freq_cols = 3 * rows, width + 128
    half = freq_cols // 2
    reach = (size - 1) // 2
    omega = math.pi * (2 * np.arange(half) + 1) / freq_cols
    across = np.arange(width)[:, None] * omega[None, :]
    col = np.concatenate([np.cos(across), -np.sin(across)], 1)
    back = col.T * (2.0 / (freq_cols * freq_rows))
    across_k = (np.arange(size + 1) - reach)[:, None] * omega[None, :]
    col_k = np.concatenate([np.cos(across_k), -np.sin(across_k)], 1)
    u = np.arange(freq_rows)
    down = 2 * math.pi / freq_rows * (u[:, None] * u[None, :] % freq_rows)
    row = np.concatenate([np.cos(down), np.sin(down)], 0)
    down_k = 2 * math.pi / freq_rows * (u[:, None] * (np.arange(size + 1) - reach)[None, :] % freq_rows)
    row_k = np.concatenate([np.cos(down_k), np.sin(down_k)], 0)
    return [halves(t) for t in (col, back, col_k, row, row_k)]


def split(x):
    high = x.astype(bf16)
    return high, (x - high.astype(f32)).astype(bf16)


def product(a, b):
    left = jnp.concatenate([a[0], a[1], a[0]], axis=1)
    right = jnp.concatenate([b[0], b[0], b[1]], axis=0)
    return jnp.dot(left, right, preferred_element_type=f32)


def turned(a, sign):
    m, n = a.shape[0] // 2, a.shape[1] // 2
    real = a[:m, :n] + sign * a[m:, n:]
    imaginary = a[:m, n:] - sign * a[m:, :n]
    return real, imaginary


def kernel(
    steps,
    nx,
    strips,
    volume_hbm,
    spread_hbm,
    measured_hbm,
    col_hbm,
    back_hbm,
    col_k_hbm,
    row_hbm,
    row_k_hbm,
    next_ref,
    residual_ref,
    volume_ref,
    spread_ref,
    measured_ref,
    col_ref,
    back_ref,
    col_k_ref,
    row_ref,
    row_k_ref,
    pad_ref,
    optic_ref,
    mid_ref,
    part_ref,
    pair_ref,
    held_ref,
    beside_ref,
    own_ref,
    piece_ref,
    full_ref,
    load_sems,
    pair_sems,
    tile_sems,
    piece_sems,
    final_sems,
    half_sems,
    halo_sems,
    relay_sems,
):
    depth, tile = lax.axis_index("depth"), lax.axis_index("tile")
    chip, core = depth // 2, depth % 2
    x, y = chip // 2, chip % 2
    partner = chip * 2 + (1 - core)
    above, below = (tile + 1) % strips, (tile + strips - 1) % strips
    chips = len(steps)
    targets = [(x + dx) % nx * 2 + (y + dy) % 2 for dx, dy in steps]
    sources = [(x + nx - dx) % nx * 2 + (y + dy) % 2 for dx, dy in steps]
    planes, rows, width = volume_ref.shape
    size = spread_ref.shape[0]
    half_rows = rows // 2
    length = half_rows // chips
    freq_rows, freq_cols = 3 * rows, width + 128
    half = freq_cols // 2

    loads = {}
    order = ("spread", "col_k", "volume", "col", "row_k", "row", "back", "measured")
    refs = {
        "spread": (spread_hbm, spread_ref),
        "col_k": (col_k_hbm, col_k_ref),
        "volume": (volume_hbm, volume_ref),
        "col": (col_hbm, col_ref),
        "row_k": (row_k_hbm, row_k_ref),
        "row": (row_hbm, row_ref),
        "back": (back_hbm, back_ref),
        "measured": (measured_hbm, measured_ref),
    }
    for i, name in enumerate(order):
        loads[name] = pltpu.make_async_copy(*refs[name], load_sems.at[i])
        loads[name].start()

    barrier = pltpu.get_barrier_semaphore()
    peers = [(partner, tile), (depth, above), (depth, below)] + [(t * 2 + core, tile) for t in targets[1:]]
    for d, t in peers:
        pl.semaphore_signal(barrier, inc=1, device_id=(d, t), device_id_type=MESH)

    sends = []

    def remote(src, dst, sems, index, d, t):
        copy = pltpu.make_async_remote_copy(
            src_ref=src,
            dst_ref=dst,
            send_sem=sems.at[(0, *index)],
            recv_sem=sems.at[(1, *index)],
            device_id=(d, t),
            device_id_type=MESH,
        )
        copy.start()
        sends.append(copy)
        return copy

    def pair(ref, *index):
        return ref[(0, *index)], ref[(1, *index)]

    pad_ref[...] = jnp.zeros_like(pad_ref)
    loads["spread"].wait()
    for d in range(planes):
        pad_ref[d, 0:size, 0:size] = spread_ref[:, d, :]
    stacked = pad_ref[...].reshape(planes * (size + 1), size + 1)
    loads["col_k"].wait()
    optic_cols = product(split(stacked), pair(col_k_ref))
    loads["volume"].wait()
    loads["col"].wait()
    plane_cols = product(split(volume_ref[...].reshape(planes * rows, width)), pair(col_ref))
    loads["row_k"].wait()
    for d in range(planes):
        optic = split(optic_cols[d * (size + 1) : (d + 1) * (size + 1)])
        real, imaginary = turned(product(pair(row_k_ref), optic), 1.0)
        optic_ref[d, 0], optic_ref[d, 1] = real, imaginary
    loads["row"].wait()
    for d in range(planes):
        plane = split(plane_cols[d * rows : (d + 1) * rows])
        row_part = pair(row_ref, slice(None), slice(0, rows))
        real, imaginary = turned(product(row_part, plane), 1.0)
        optic_real, optic_imaginary = optic_ref[d, 0], optic_ref[d, 1]
        sum_real = optic_real * real - optic_imaginary * imaginary
        sum_imaginary = optic_real * imaginary + optic_imaginary * real
        if d == 0:
            mid_ref[0], mid_ref[1] = sum_real, sum_imaginary
        else:
            mid_ref[0] += sum_real
            mid_ref[1] += sum_imaginary
    total = split(jnp.concatenate([mid_ref[0], mid_ref[1]], axis=1))

    def strips_of(first, count):
        ends = [
            jnp.concatenate(
                [row_ref[p, k * freq_rows + first * rows : k * freq_rows + (first + count) * rows] for k in range(2)], axis=0
            )
            for p in range(2)
        ]
        real, imaginary = turned(product(ends, total), -1.0)
        mixed = jnp.concatenate([real, imaginary], axis=1)
        part = product(split(mixed), pair(back_ref))
        part_ref[first : first + count] = part.reshape(count, 2, half_rows, width)

    def to_partner(b):
        return remote(part_ref.at[b, 1 - core], pair_ref.at[b], pair_sems, (b,), partner, tile)

    loads["back"].wait()
    strips_of(1, 2)
    pl.semaphore_wait(barrier, len(peers))
    paired = {b: to_partner(b) for b in (1, 2)}
    strips_of(0, 1)
    paired[0] = to_partner(0)

    near = {}
    for b in (1, 2):
        paired[b].wait_recv()
        held_ref[b - 1] = (part_ref[b, core] + pair_ref[b]).reshape(chips, length, width)
    for i in reversed(range(chips)):
        for b, t in ((0, above), (1, below)):
            near[b, i] = remote(held_ref.at[b, targets[i]], beside_ref.at[b, i], tile_sems, (b, i), depth, t)
    paired[0].wait_recv()
    own_ref[...] = (part_ref[0, core] + pair_ref[0]).reshape(chips, length, width)

    pieces = {}
    for i in reversed(range(chips)):
        near[0, i].wait_recv()
        near[1, i].wait_recv()
        value = own_ref[targets[i]]
        value += jnp.where(tile > 0, beside_ref[0, i], 0.0)
        value += jnp.where(tile < strips - 1, beside_ref[1, i], 0.0)
        if i:
            held_ref[2, i] = value
            pieces[i] = remote(held_ref.at[2, i], piece_ref.at[i], piece_sems, (i,), targets[i] * 2 + core, tile)
    loads["measured"].wait()
    start = pl.multiple_of(core * half_rows + chip * length, length)
    value -= measured_ref[pl.ds(start, length), :]
    for i in range(1, chips):
        pieces[i].wait_recv()
        value += piece_ref[i]
    full_ref[0, core, chip] = value

    finals, halos, halved, relayed = {}, {}, {}, {}
    mine = full_ref.at[0, core, chip]
    for i in reversed(range(1, chips)):
        finals[i] = remote(mine, mine, final_sems, (i,), targets[i] * 2 + core, tile)
    for i in range(chips):
        j = sources[i]
        here = full_ref.at[0, core, j]
        if i:
            finals[i].wait_recv()
        halos[0, i] = remote(here, full_ref.at[2, core, j], halo_sems, (0, i), depth, above)
        halos[1, i] = remote(here, full_ref.at[1, core, j], halo_sems, (1, i), depth, below)
        halved[i] = remote(here, here, half_sems, (i,), partner, tile)
    for i in range(chips):
        for b, block in ((0, 2), (1, 1)):
            halos[b, i].wait_recv()
            there = full_ref.at[block, core, sources[i]]
            relayed[b, i] = remote(there, there, relay_sems, (b, i), partner, tile)
    for i in range(chips):
        halved[i].wait_recv()
    strip = full_ref[0].reshape(rows, width)
    residual_ref[...] = strip
    for i in range(chips):
        for b in (0, 1):
            relayed[b, i].wait_recv()
    after = jnp.where(tile < strips - 1, full_ref[1].reshape(rows, width), 0.0)
    before = jnp.where(tile > 0, full_ref[2].reshape(rows, width), 0.0)
    block = jnp.concatenate([strip, after, before], axis=0)
    block_cols = product(split(block), pair(col_ref))
    real, imaginary = turned(product(pair(row_ref), split(block_cols)), 1.0)
    mid_ref[0], mid_ref[1] = real, imaginary
    for d in range(planes):
        real, imaginary = mid_ref[0], mid_ref[1]
        optic_real, optic_imaginary = optic_ref[d, 0], optic_ref[d, 1]
        grad_real = optic_real * real + optic_imaginary * imaginary
        grad_imaginary = optic_real * imaginary - optic_imaginary * real
        grad = split(jnp.concatenate([grad_real, grad_imaginary], axis=1))
        ends = [jnp.concatenate([row_ref[p, 0:rows], row_ref[p, freq_rows : freq_rows + rows]], axis=0) for p in range(2)]
        real, imaginary = turned(product(ends, grad), -1.0)
        mixed = split(jnp.concatenate([real, imaginary], axis=1))
        gradient = product(mixed, pair(back_ref))
        shifted = volume_ref[d] - step_size * gradient
        next_ref[d] = shifted - jnp.clip(shifted, -threshold, threshold)
    for copy in sends:
        copy.wait_send()


def finish(next_ref, residual_ref, next_out, residual_out):
    next_out[...] = next_ref[...]
    residual_out[...] = residual_ref[...]


def per_device(volume, point_spread, measured):
    planes, rows, width = volume.shape
    size = point_spread.shape[1]
    chips, strips = lax.axis_size("depth") // 2, lax.axis_size("tile")
    nx = chips // 2
    steps = sorted(((dx, dy) for dx in range(nx) for dy in range(2)), key=lambda s: (min(s[0], nx - s[0]) + 2 * s[1], s))
    constants = [jnp.asarray(t) for t in tables(rows, width, size)]
    spread = jnp.transpose(point_spread, (1, 0, 2))
    half_rows = rows // 2
    length = half_rows // chips
    freq_rows, half = 3 * rows, (width + 128) // 2
    vmem = pl.BlockSpec(memory_space=pltpu.VMEM)
    dma = pltpu.SemaphoreType.DMA
    inputs = (volume, spread, measured, *constants)
    shapes = (jax.ShapeDtypeStruct((planes, rows, width), f32), jax.ShapeDtypeStruct((rows, width), f32))
    outs = pl.pallas_call(
        functools.partial(kernel, steps, nx, strips),
        out_shape=shapes,
        in_specs=[pl.BlockSpec(memory_space=pltpu.HBM)] * 8,
        out_specs=(vmem, vmem),
        scratch_shapes=[pltpu.VMEM(a.shape, a.dtype) for a in inputs]
        + [
            pltpu.VMEM((planes, size + 1, size + 1), f32),
            pltpu.VMEM((planes, 2, freq_rows, half), f32),
            pltpu.VMEM((2, freq_rows, half), f32),
            pltpu.VMEM((3, 2, half_rows, width), f32),
            pltpu.VMEM((3, half_rows, width), f32),
            pltpu.VMEM((3, chips, length, width), f32),
            pltpu.VMEM((2, chips, length, width), f32),
            pltpu.VMEM((chips, length, width), f32),
            pltpu.VMEM((chips, length, width), f32),
            pltpu.VMEM((3, 2, chips, length, width), f32),
            dma((8,)),
            dma((2, 3)),
            dma((2, 2, chips)),
            dma((2, chips)),
            dma((2, chips)),
            dma((2, chips)),
            dma((2, 2, chips)),
            dma((2, 2, chips)),
        ],
        compiler_params=pltpu.CompilerParams(
            collective_id=0, has_side_effects=True, vmem_limit_bytes=24 * 2**20
        ),
    )(*inputs)
    return pl.pallas_call(
        finish,
        out_shape=shapes,
        in_specs=[vmem, vmem],
        out_specs=(vmem, vmem),
        compiler_params=pltpu.CompilerParams(vmem_limit_bytes=8 * 2**20),
    )(*outs)


def solution(mesh):
    placed = (P("depth", "tile", None), P("depth", None, None), P("tile", None))
    return jax.shard_map(
        per_device,
        mesh=mesh,
        in_specs=placed,
        out_specs=(P("depth", "tile", None), P("tile", None)),
        check_vma=False,
    )
```

```python
import functools
import math

import jax
import jax.numpy as jnp
import ml_dtypes
import numpy as np
from jax import lax
from jax.experimental import pallas as pl
from jax.experimental.pallas import tpu as pltpu
from jax.sharding import PartitionSpec as P

step_size = 2.0
threshold = 0.5
f32 = jnp.float32
bf16 = jnp.bfloat16
MESH = pl.DeviceIdType.MESH


def halves(table):
    table = table.astype(np.float32)
    high = table.astype(ml_dtypes.bfloat16)
    low = (table - high.astype(np.float32)).astype(ml_dtypes.bfloat16)
    return np.stack([high, low])


def tables(rows, width, size):
    freq_rows, freq_cols = 3 * rows, width + 128
    reach = (size - 1) // 2
    omega = math.pi * (2 * np.arange(freq_cols // 2) + 1) / freq_cols
    across = np.arange(width)[:, None] * omega[None, :]
    col = np.concatenate([np.cos(across), -np.sin(across)], 1)
    back = col.T * (2.0 / (freq_cols * freq_rows))
    across_k = (np.arange(size + 1) - reach)[:, None] * omega[None, :]
    col_k = np.concatenate([np.cos(across_k), -np.sin(across_k)], 1)
    theta = math.pi * (2 * np.arange(freq_rows // 2) + 1) / freq_rows
    place = np.concatenate([np.arange(2 * rows), np.arange(-rows, 0)])
    down = theta[:, None] * place[None, :]
    row = np.concatenate([np.cos(down), np.sin(down)], 0)
    down_k = theta[:, None] * (np.arange(size + 1) - reach)[None, :]
    row_k = np.concatenate([np.cos(down_k), np.sin(down_k)], 0)
    return [halves(t) for t in (col, back, col_k, row, row.T, row_k)]


def split(x):
    high = x.astype(bf16)
    return high, (x - high.astype(f32)).astype(bf16)


def product(a, b):
    left = jnp.concatenate([a[0], a[1], a[0]], axis=1)
    right = jnp.concatenate([b[0], b[0], b[1]], axis=0)
    return jnp.dot(left, right, preferred_element_type=f32)


def spectrum(a):
    m, n = a.shape[0] // 2, a.shape[1] // 2
    cos_real, cos_imaginary, sin_real, sin_imaginary = a[:m, :n], a[:m, n:], a[m:, :n], a[m:, n:]
    return (
        cos_real + sin_imaginary,
        cos_imaginary - sin_real,
        cos_real - sin_imaginary,
        cos_imaginary + sin_real,
    )


def folded(plus_real, plus_imaginary, minus_real, minus_imaginary):
    even = jnp.concatenate([plus_real + minus_real, plus_imaginary + minus_imaginary], axis=1)
    odd = jnp.concatenate([minus_imaginary - plus_imaginary, plus_real - minus_real], axis=1)
    return jnp.concatenate([even, odd], axis=0)


def kernel(
    steps,
    nx,
    strips,
    volume_hbm,
    spread_hbm,
    measured_hbm,
    col_hbm,
    back_hbm,
    col_k_hbm,
    row_hbm,
    row_back_hbm,
    row_k_hbm,
    next_ref,
    residual_ref,
    volume_ref,
    spread_ref,
    measured_ref,
    col_ref,
    back_ref,
    col_k_ref,
    row_ref,
    row_back_ref,
    row_k_ref,
    pad_ref,
    optic_ref,
    sum_ref,
    part_ref,
    pair_ref,
    held_ref,
    beside_ref,
    own_ref,
    block_ref,
    piece_ref,
    full_ref,
    load_sems,
    pair_sems,
    tile_sems,
    piece_sems,
    final_sems,
    half_sems,
    halo_sems,
):
    depth, tile = lax.axis_index("depth"), lax.axis_index("tile")
    chip, core = depth // 2, depth % 2
    x, y = chip // 2, chip % 2
    partner = chip * 2 + (1 - core)
    above, below = (tile + 1) % strips, (tile + strips - 1) % strips
    chips = len(steps)
    targets = [(x + dx) % nx * 2 + (y + dy) % 2 for dx, dy in steps]
    sources = [(x + nx - dx) % nx * 2 + (y + dy) % 2 for dx, dy in steps]
    planes, rows, width = volume_ref.shape
    size = spread_ref.shape[0]
    half_rows = rows // 2
    length = half_rows // chips
    freq_rows, freq_cols = 3 * rows, width + 128
    loads = {}
    order = ("spread", "col_k", "volume", "col", "row_k", "row", "row_back", "back", "measured")
    refs = {
        "spread": (spread_hbm, spread_ref),
        "col_k": (col_k_hbm, col_k_ref),
        "volume": (volume_hbm, volume_ref),
        "col": (col_hbm, col_ref),
        "row_k": (row_k_hbm, row_k_ref),
        "row": (row_hbm, row_ref),
        "row_back": (row_back_hbm, row_back_ref),
        "back": (back_hbm, back_ref),
        "measured": (measured_hbm, measured_ref),
    }
    for i, name in enumerate(order):
        loads[name] = pltpu.make_async_copy(*refs[name], load_sems.at[i])
    for name in order[:4]:
        loads[name].start()

    barrier = pltpu.get_barrier_semaphore()
    peers = [(partner, tile)] + [(d, t) for t in (above, below) for d in (depth, partner)]
    peers += [(t * 2 + core, tile) for t in targets[1:]]
    for d, t in peers:
        pl.semaphore_signal(barrier, inc=1, device_id=(d, t), device_id_type=MESH)

    sends = []

    def remote(src, dst, sems, index, d, t):
        copy = pltpu.make_async_remote_copy(
            src_ref=src,
            dst_ref=dst,
            send_sem=sems.at[(0, *index)],
            recv_sem=sems.at[(1, *index)],
            device_id=(d, t),
            device_id_type=MESH,
        )
        copy.start()
        sends.append(copy)
        return copy

    def pair(ref, *index):
        return ref[(0, *index)], ref[(1, *index)]

    pad_ref[...] = jnp.zeros_like(pad_ref)
    loads["spread"].wait()
    for d in range(planes):
        pad_ref[d, 0:size, 0:size] = spread_ref[:, d, :]
    stacked = pad_ref[...].reshape(planes * (size + 1), size + 1)
    loads["col_k"].wait()
    for name in order[4:6]:
        loads[name].start()
    optic_cols = product(split(stacked), pair(col_k_ref))
    loads["volume"].wait()
    loads["col"].wait()
    for name in order[6:]:
        loads[name].start()
    plane_cols = product(split(volume_ref[...].reshape(planes * rows, width)), pair(col_ref))
    loads["row_k"].wait()
    for d in range(planes):
        optic = split(optic_cols[d * (size + 1) : (d + 1) * (size + 1)])
        for k, value in enumerate(spectrum(product(pair(row_k_ref), optic))):
            optic_ref[d, k] = value
    loads["row"].wait()
    for d in range(planes):
        plane = split(plane_cols[d * rows : (d + 1) * rows])
        values = spectrum(product(pair(row_ref, slice(None), slice(0, rows)), plane))
        for k in (0, 2):
            optic_real, optic_imaginary = optic_ref[d, k], optic_ref[d, k + 1]
            real, imaginary = values[k], values[k + 1]
            sum_real = optic_real * real - optic_imaginary * imaginary
            sum_imaginary = optic_real * imaginary + optic_imaginary * real
            if d == 0:
                sum_ref[k], sum_ref[k + 1] = sum_real, sum_imaginary
            else:
                sum_ref[k] += sum_real
                sum_ref[k + 1] += sum_imaginary
    total = split(folded(*(sum_ref[k] for k in range(4))))

    def strips_of(first, count):
        part_rows = pair(row_back_ref, slice(first * rows, (first + count) * rows))
        part = product(split(product(part_rows, total)), pair(back_ref))
        part_ref[first : first + count] = part.reshape(count, 2, half_rows, width)

    def to_partner(b):
        return remote(part_ref.at[b, 1 - core], pair_ref.at[b], pair_sems, (b,), partner, tile)

    loads["row_back"].wait()
    loads["back"].wait()
    strips_of(1, 2)
    pl.semaphore_wait(barrier, len(peers))
    paired = {b: to_partner(b) for b in (1, 2)}
    strips_of(0, 1)
    paired[0] = to_partner(0)

    near = {}
    for b in (1, 2):
        paired[b].wait_recv()
        held_ref[b - 1] = (part_ref[b, core] + pair_ref[b]).reshape(chips, length, width)
    for i in reversed(range(chips)):
        for b, t in ((0, above), (1, below)):
            near[b, i] = remote(held_ref.at[b, targets[i]], beside_ref.at[b, i], tile_sems, (b, i), depth, t)
    paired[0].wait_recv()
    own_ref[...] = (part_ref[0, core] + pair_ref[0]).reshape(chips, length, width)

    pieces = {}
    for i in reversed(range(chips)):
        near[0, i].wait_recv()
        near[1, i].wait_recv()
        value = own_ref[targets[i]]
        value += jnp.where(tile > 0, beside_ref[0, i], 0.0)
        value += jnp.where(tile < strips - 1, beside_ref[1, i], 0.0)
        if i:
            held_ref[2, i] = value
            pieces[i] = remote(held_ref.at[2, i], piece_ref.at[i], piece_sems, (i,), targets[i] * 2 + core, tile)
    loads["measured"].wait()
    start = pl.multiple_of(core * half_rows + chip * length, length)
    value -= measured_ref[pl.ds(start, length), :]
    for i in range(1, chips):
        pieces[i].wait_recv()
        value += piece_ref[i]
    full_ref[0, core, chip] = value

    finals, halos, halved = {}, {}, {}
    mine = full_ref.at[0, core, chip]
    for i in reversed(range(1, chips)):
        finals[i] = remote(mine, mine, final_sems, (i,), targets[i] * 2 + core, tile)
    for i in range(chips):
        j = sources[i]
        here = full_ref.at[0, core, j]
        if i:
            finals[i].wait_recv()
        halved[i] = remote(here, here, half_sems, (i,), partner, tile)
        for c, d in ((0, depth), (1, partner)):
            halos[0, c, i] = remote(here, full_ref.at[2, core, j], halo_sems, (0, c, i), d, above)
            halos[1, c, i] = remote(here, full_ref.at[1, core, j], halo_sems, (1, c, i), d, below)
    for i in range(chips):
        halved[i].wait_recv()

    strip = full_ref[0].reshape(rows, width)
    residual_ref[...] = strip
    strip_cols = split(product(split(strip), pair(col_ref)))
    block_ref[...] = product(pair(row_ref, slice(None), slice(0, rows)), strip_cols)
    for i in range(chips):
        for b in (0, 1):
            for c in (0, 1):
                halos[b, c, i].wait_recv()
    after = jnp.where(tile < strips - 1, full_ref[1].reshape(rows, width), 0.0)
    before = jnp.where(tile > 0, full_ref[2].reshape(rows, width), 0.0)
    beside_cols = split(product(split(jnp.concatenate([after, before], axis=0)), pair(col_ref)))
    block_ref[...] += product(pair(row_ref, slice(None), slice(rows, freq_rows)), beside_cols)
    mixed = []
    for d in range(planes):
        values = spectrum(block_ref[...])
        grad = []
        for k in (0, 2):
            optic_real, optic_imaginary = optic_ref[d, k], optic_ref[d, k + 1]
            real, imaginary = values[k], values[k + 1]
            grad.append(optic_real * real + optic_imaginary * imaginary)
            grad.append(optic_real * imaginary - optic_imaginary * real)
        mixed.append(product(pair(row_back_ref, slice(0, rows)), split(folded(*grad))))
    gradient = product(split(jnp.concatenate(mixed, axis=0)), pair(back_ref)).reshape(planes, rows, width)
    shifted = volume_ref[...] - step_size * gradient
    next_ref[...] = shifted - jnp.clip(shifted, -threshold, threshold)
    for copy in sends:
        copy.wait_send()


def finish(next_ref, residual_ref, next_out, residual_out):
    next_out[...] = next_ref[...]
    residual_out[...] = residual_ref[...]


def per_device(volume, point_spread, measured):
    planes, rows, width = volume.shape
    size = point_spread.shape[1]
    chips, strips = lax.axis_size("depth") // 2, lax.axis_size("tile")
    nx = chips // 2
    steps = sorted(((dx, dy) for dx in range(nx) for dy in range(2)), key=lambda s: (min(s[0], nx - s[0]) + 2 * s[1], s))
    constants = [jnp.asarray(t) for t in tables(rows, width, size)]
    spread = jnp.transpose(point_spread, (1, 0, 2))
    half_rows = rows // 2
    length = half_rows // chips
    freq_rows, half = 3 * rows, (width + 128) // 2
    vmem = pl.BlockSpec(memory_space=pltpu.VMEM)
    dma = pltpu.SemaphoreType.DMA
    inputs = tuple(pltpu.with_memory_space_constraint(a, pltpu.HBM) for a in (volume, spread, measured, *constants))
    shapes = (jax.ShapeDtypeStruct((planes, rows, width), f32), jax.ShapeDtypeStruct((rows, width), f32))
    outs = pl.pallas_call(
        functools.partial(kernel, steps, nx, strips),
        out_shape=shapes,
        in_specs=[pl.BlockSpec(memory_space=pl.ANY)] * 9,
        out_specs=(vmem, vmem),
        scratch_shapes=[pltpu.VMEM(a.shape, a.dtype) for a in inputs]
        + [
            pltpu.VMEM((planes, size + 1, size + 1), f32),
            pltpu.VMEM((planes, 4, freq_rows // 2, half), f32),
            pltpu.VMEM((4, freq_rows // 2, half), f32),
            pltpu.VMEM((3, 2, half_rows, width), f32),
            pltpu.VMEM((3, half_rows, width), f32),
            pltpu.VMEM((3, chips, length, width), f32),
            pltpu.VMEM((2, chips, length, width), f32),
            pltpu.VMEM((chips, length, width), f32),
            pltpu.VMEM((freq_rows, 2 * half), f32),
            pltpu.VMEM((chips, length, width), f32),
            pltpu.VMEM((3, 2, chips, length, width), f32),
            dma((9,)),
            dma((2, 3)),
            dma((2, 2, chips)),
            dma((2, chips)),
            dma((2, chips)),
            dma((2, chips)),
            dma((2, 2, 2, chips)),
        ],
        compiler_params=pltpu.CompilerParams(
            collective_id=0, has_side_effects=True, vmem_limit_bytes=20 * 2**20
        ),
    )(*inputs)
    return pl.pallas_call(
        finish,
        out_shape=shapes,
        in_specs=[vmem, vmem],
        out_specs=(vmem, vmem),
        compiler_params=pltpu.CompilerParams(vmem_limit_bytes=8 * 2**20),
    )(*outs)


def solution(mesh):
    placed = (P("depth", "tile", None), P("depth", None, None), P("tile", None))
    return jax.shard_map(
        per_device,
        mesh=mesh,
        in_specs=placed,
        out_specs=(P("depth", "tile", None), P("tile", None)),
        check_vma=False,
    )
```

```python
import functools
import math

import jax
import jax.numpy as jnp
import ml_dtypes
import numpy as np
from jax import lax
from jax.experimental import pallas as pl
from jax.experimental.pallas import tpu as pltpu
from jax.sharding import PartitionSpec as P

step_size = 2.0
threshold = 0.5
f32 = jnp.float32
bf16 = jnp.bfloat16
MESH = pl.DeviceIdType.MESH


def halves(table):
    table = table.astype(np.float32)
    high = table.astype(ml_dtypes.bfloat16)
    low = (table - high.astype(np.float32)).astype(ml_dtypes.bfloat16)
    return np.stack([high, low])


def tables(rows, width, size):
    freq_rows, freq_cols = 3 * rows, width + 128
    reach = (size - 1) // 2
    omega = math.pi * (2 * np.arange(freq_cols // 2) + 1) / freq_cols
    across = np.arange(width)[:, None] * omega[None, :]
    col = np.concatenate([np.cos(across), -np.sin(across)], 1)
    back = col.T * (2.0 / (freq_cols * freq_rows))
    across_k = (np.arange(size + 1) - reach)[:, None] * omega[None, :]
    col_k = np.concatenate([np.cos(across_k), -np.sin(across_k)], 1)
    theta = math.pi * (2 * np.arange(freq_rows // 2) + 1) / freq_rows
    place = np.concatenate([np.arange(2 * rows), np.arange(-rows, 0)])
    down = theta[:, None] * place[None, :]
    row = np.concatenate([np.cos(down), np.sin(down)], 0)
    down_k = theta[:, None] * (np.arange(size + 1) - reach)[None, :]
    row_k = np.concatenate([np.cos(down_k), np.sin(down_k)], 0)
    return [halves(t) for t in (col, back, col_k, row, row.T, row_k)]


def split(x):
    high = x.astype(bf16)
    return high, (x - high.astype(f32)).astype(bf16)


def product(a, b):
    left = jnp.concatenate([a[0], a[1], a[0]], axis=1)
    right = jnp.concatenate([b[0], b[0], b[1]], axis=0)
    return jnp.dot(left, right, preferred_element_type=f32)


def spectrum(a):
    m, n = a.shape[0] // 2, a.shape[1] // 2
    cos_real, cos_imaginary, sin_real, sin_imaginary = a[:m, :n], a[:m, n:], a[m:, :n], a[m:, n:]
    return (
        cos_real + sin_imaginary,
        cos_imaginary - sin_real,
        cos_real - sin_imaginary,
        cos_imaginary + sin_real,
    )


def folded(plus_real, plus_imaginary, minus_real, minus_imaginary):
    even = jnp.concatenate([plus_real + minus_real, plus_imaginary + minus_imaginary], axis=1)
    odd = jnp.concatenate([minus_imaginary - plus_imaginary, plus_real - minus_real], axis=1)
    return jnp.concatenate([even, odd], axis=0)


def when(condition, action):
    if condition is None:
        action()
    else:
        pl.when(condition)(action)


def kernel(
    steps,
    nx,
    strips,
    volume_hbm,
    spread_hbm,
    measured_hbm,
    col_hbm,
    back_hbm,
    col_k_hbm,
    row_hbm,
    row_back_hbm,
    row_k_hbm,
    next_ref,
    residual_ref,
    volume_ref,
    spread_ref,
    measured_ref,
    col_ref,
    back_ref,
    col_k_ref,
    row_ref,
    row_back_ref,
    row_k_ref,
    pad_ref,
    optic_ref,
    sum_ref,
    part_ref,
    pair_ref,
    held_ref,
    beside_ref,
    own_ref,
    block_ref,
    piece_ref,
    full_ref,
    load_sems,
    pair_sems,
    tile_sems,
    piece_sems,
    final_sems,
    half_sems,
    halo_sems,
):
    depth, tile = lax.axis_index("depth"), lax.axis_index("tile")
    chip, core = depth // 2, depth % 2
    x, y = chip // 2, chip % 2
    partner = chip * 2 + (1 - core)
    above, below = (tile + 1) % strips, (tile + strips - 1) % strips
    has_above, has_below = tile < strips - 1, tile > 0
    chips = len(steps)
    hops = [min(dx, nx - dx) + 2 * dy for dx, dy in steps]
    far = [i for i in range(chips) if hops[i] >= 2]
    far_out = [i for i in range(chips) if hops[i] >= 1]
    targets = [(x + dx) % nx * 2 + (y + dy) % 2 for dx, dy in steps]
    sources = [(x + nx - dx) % nx * 2 + (y + dy) % 2 for dx, dy in steps]
    planes, rows, width = volume_ref.shape
    size = spread_ref.shape[0]
    half_rows = rows // 2
    length = half_rows // chips
    freq_rows, freq_cols = 3 * rows, width + 128
    loads = {}
    order = ("spread", "col_k", "volume", "col", "row_k", "row", "row_back", "back", "measured")
    refs = {
        "spread": (spread_hbm, spread_ref),
        "col_k": (col_k_hbm, col_k_ref),
        "volume": (volume_hbm, volume_ref),
        "col": (col_hbm, col_ref),
        "row_k": (row_k_hbm, row_k_ref),
        "row": (row_hbm, row_ref),
        "row_back": (row_back_hbm, row_back_ref),
        "back": (back_hbm, back_ref),
        "measured": (measured_hbm, measured_ref),
    }
    for i, name in enumerate(order):
        loads[name] = pltpu.make_async_copy(*refs[name], load_sems.at[i])
    for name in order:
        loads[name].start()

    barrier = pltpu.get_barrier_semaphore()
    inside = [partner] + [t * 2 + core for t in targets[1:]]
    across = [depth, partner] + [targets[i] * 2 + core for i in sorted({*far, *far_out})]

    def greet(devices, t):
        for d in devices:
            pl.semaphore_signal(barrier, inc=1, device_id=(d, t), device_id_type=MESH)

    greet(inside, tile)
    when(has_above, lambda: greet(across, above))
    when(has_below, lambda: greet(across, below))
    arrivals = len(inside) + sum(jnp.where(side, len(across), 0) for side in (has_above, has_below))

    sends = []

    def remote(src, dst, sems, index, d, t, going=None, coming=None):
        copy = pltpu.make_async_remote_copy(
            src_ref=src,
            dst_ref=dst,
            send_sem=sems.at[(0, *index)],
            recv_sem=sems.at[(1, *index)],
            device_id=(d, t),
            device_id_type=MESH,
        )
        when(going, copy.start)
        sends.append(lambda: when(going, copy.wait_send))
        return lambda: when(coming, copy.wait_recv)

    sides = ((above, has_above, has_below), (below, has_below, has_above))

    def pair(ref, *index):
        return ref[(0, *index)], ref[(1, *index)]

    pad_ref[...] = jnp.zeros_like(pad_ref)
    loads["spread"].wait()
    for d in range(planes):
        pad_ref[d, 0:size, 0:size] = spread_ref[:, d, :]
    loads["col_k"].wait()
    stacked = pad_ref[...].reshape(planes * (size + 1), size + 1)
    optic_cols = product(split(stacked), pair(col_k_ref))
    loads["volume"].wait()
    loads["col"].wait()
    loads["row_k"].wait()
    loads["row"].wait()
    optic = split(optic_cols[0 * (size + 1) : (0 + 1) * (size + 1)])
    for k, value in enumerate(spectrum(product(pair(row_k_ref), optic))):
        optic_ref[0, k] = value
    plane_cols = product(split(volume_ref[...].reshape(planes * rows, width)), pair(col_ref))
    plane = split(plane_cols[0 * rows : (0 + 1) * rows])
    values = spectrum(product(pair(row_ref, slice(None), slice(0, rows)), plane))
    for k in (0, 2):
        optic_real, optic_imaginary = optic_ref[0, k], optic_ref[0, k + 1]
        real, imaginary = values[k], values[k + 1]
        sum_real = optic_real * real - optic_imaginary * imaginary
        sum_imaginary = optic_real * imaginary + optic_imaginary * real
        sum_ref[k], sum_ref[k + 1] = sum_real, sum_imaginary
    optic = split(optic_cols[1 * (size + 1) : (1 + 1) * (size + 1)])
    for k, value in enumerate(spectrum(product(pair(row_k_ref), optic))):
        optic_ref[1, k] = value
    plane = split(plane_cols[1 * rows : (1 + 1) * rows])
    values = spectrum(product(pair(row_ref, slice(None), slice(0, rows)), plane))
    for k in (0, 2):
        optic_real, optic_imaginary = optic_ref[1, k], optic_ref[1, k + 1]
        real, imaginary = values[k], values[k + 1]
        sum_real = optic_real * real - optic_imaginary * imaginary
        sum_imaginary = optic_real * imaginary + optic_imaginary * real
        sum_ref[k] += sum_real
        sum_ref[k + 1] += sum_imaginary
    total = split(folded(*(sum_ref[k] for k in range(4))))

    def strips_of(first, count):
        part_rows = pair(row_back_ref, slice(first * rows, (first + count) * rows))
        part = product(split(product(part_rows, total)), pair(back_ref))
        part_ref[first : first + count] = part.reshape(count, 2, half_rows, width)

    def to_partner(b):
        return remote(part_ref.at[b, 1 - core], pair_ref.at[b], pair_sems, (b,), partner, tile)

    loads["row_back"].wait()
    loads["back"].wait()
    strips_of(1, 2)
    pl.semaphore_wait(barrier, arrivals)
    paired = {b: to_partner(b) for b in (1, 2)}
    strips_of(0, 1)
    paired[0] = to_partner(0)

    near = {}
    for b in (1, 2):
        paired[b]()
        held_ref[b - 1] = (part_ref[b, core] + pair_ref[b]).reshape(chips, length, width)
    for i in reversed(range(chips)):
        for b, side in enumerate(sides):
            to = targets[i] * 2 + core if i in far else depth
            near[b, i] = remote(held_ref.at[b, targets[i]], beside_ref.at[b, i], tile_sems, (b, i), to, *side)
    paired[0]()
    own_ref[...] = (part_ref[0, core] + pair_ref[0]).reshape(chips, length, width)

    pieces = {}

    def from_beside(i):
        near[0, i]()
        near[1, i]()
        value = jnp.where(has_below, beside_ref[0, i], 0.0)
        return value + jnp.where(has_above, beside_ref[1, i], 0.0)

    for i in far:
        pieces[i] = remote(own_ref.at[targets[i]], piece_ref.at[i], piece_sems, (i,), targets[i] * 2 + core, tile)
    for i in reversed(range(chips)):
        if i in far:
            continue
        value = own_ref[targets[i]] + from_beside(i)
        if i:
            held_ref[2, i] = value
            pieces[i] = remote(held_ref.at[2, i], piece_ref.at[i], piece_sems, (i,), targets[i] * 2 + core, tile)
    loads["measured"].wait()
    start = pl.multiple_of(core * half_rows + chip * length, length)
    value -= measured_ref[pl.ds(start, length), :]
    for i in range(1, chips):
        pieces[i]()
        value += piece_ref[i]
        if i in far:
            value += from_beside(i)
    full_ref[0, core, chip] = value

    finals, halos, halved = {}, {}, {}
    mine = full_ref.at[0, core, chip]
    for i in reversed(range(1, chips)):
        to = targets[i] * 2 + core
        finals[i] = remote(mine, mine, final_sems, (i,), to, tile)
        if i in far_out:
            for b, side in enumerate(sides):
                halos[b, 0, i] = remote(mine, full_ref.at[2 - b, core, chip], halo_sems, (b, 0, i), to, *side)
    for i in range(chips):
        j = sources[i]
        here = full_ref.at[0, core, j]
        if i:
            finals[i]()
        halved[i] = remote(here, here, half_sems, (i,), partner, tile)
        if i not in far_out:
            for b, side in enumerate(sides):
                for c, d in enumerate((depth, partner)):
                    halos[b, c, i] = remote(here, full_ref.at[2 - b, core, j], halo_sems, (b, c, i), d, *side)
    for i in far_out:
        for b, (_, _, coming) in enumerate(sides):
            halos[b, 0, i]()
            there = full_ref.at[2 - b, core, sources[i]]
            halos[b, 1, i] = remote(there, there, halo_sems, (b, 1, i), partner, tile, coming, coming)
    for i in range(chips):
        halved[i]()

    strip = full_ref[0].reshape(rows, width)
    residual_ref[...] = strip
    strip_cols = split(product(split(strip), pair(col_ref)))
    block_ref[...] = product(pair(row_ref, slice(None), slice(0, rows)), strip_cols)
    for i in range(chips):
        for b in (0, 1):
            for c in (1,) if i in far_out else (0, 1):
                halos[b, c, i]()
    after = jnp.where(has_above, full_ref[1].reshape(rows, width), 0.0)
    before = jnp.where(has_below, full_ref[2].reshape(rows, width), 0.0)
    beside_cols = split(product(split(jnp.concatenate([after, before], axis=0)), pair(col_ref)))
    block_ref[...] += product(pair(row_ref, slice(None), slice(rows, freq_rows)), beside_cols)
    mixed = []
    for d in range(planes):
        values = spectrum(block_ref[...])
        grad = []
        for k in (0, 2):
            optic_real, optic_imaginary = optic_ref[d, k], optic_ref[d, k + 1]
            real, imaginary = values[k], values[k + 1]
            grad.append(optic_real * real + optic_imaginary * imaginary)
            grad.append(optic_real * imaginary - optic_imaginary * real)
        mixed.append(product(pair(row_back_ref, slice(0, rows)), split(folded(*grad))))
    gradient = product(split(jnp.concatenate(mixed, axis=0)), pair(back_ref)).reshape(planes, rows, width)
    shifted = volume_ref[...] - step_size * gradient
    next_ref[...] = shifted - jnp.clip(shifted, -threshold, threshold)
    for wait in sends:
        wait()


def finish(next_ref, residual_ref, next_out, residual_out):
    next_out[...] = next_ref[...]
    residual_out[...] = residual_ref[...]


def per_device(volume, point_spread, measured):
    planes, rows, width = volume.shape
    size = point_spread.shape[1]
    chips, strips = lax.axis_size("depth") // 2, lax.axis_size("tile")
    nx = chips // 2
    steps = sorted(((dx, dy) for dx in range(nx) for dy in range(2)), key=lambda s: (min(s[0], nx - s[0]) + 2 * s[1], s))
    constants = [jnp.asarray(t) for t in tables(rows, width, size)]
    spread = jnp.transpose(point_spread, (1, 0, 2))
    half_rows = rows // 2
    length = half_rows // chips
    freq_rows, half = 3 * rows, (width + 128) // 2
    vmem = pl.BlockSpec(memory_space=pltpu.VMEM)
    dma = pltpu.SemaphoreType.DMA
    inputs = tuple(pltpu.with_memory_space_constraint(a, pltpu.HBM) for a in (volume, spread, measured, *constants))
    shapes = (jax.ShapeDtypeStruct((planes, rows, width), f32), jax.ShapeDtypeStruct((rows, width), f32))
    outs = pl.pallas_call(
        functools.partial(kernel, steps, nx, strips),
        out_shape=shapes,
        in_specs=[pl.BlockSpec(memory_space=pl.ANY)] * 9,
        out_specs=(vmem, vmem),
        scratch_shapes=[pltpu.VMEM(a.shape, a.dtype) for a in inputs]
        + [
            pltpu.VMEM((planes, size + 1, size + 1), f32),
            pltpu.VMEM((planes, 4, freq_rows // 2, half), f32),
            pltpu.VMEM((4, freq_rows // 2, half), f32),
            pltpu.VMEM((3, 2, half_rows, width), f32),
            pltpu.VMEM((3, half_rows, width), f32),
            pltpu.VMEM((3, chips, length, width), f32),
            pltpu.VMEM((2, chips, length, width), f32),
            pltpu.VMEM((chips, length, width), f32),
            pltpu.VMEM((freq_rows, 2 * half), f32),
            pltpu.VMEM((chips, length, width), f32),
            pltpu.VMEM((3, 2, chips, length, width), f32),
            dma((9,)),
            dma((2, 3)),
            dma((2, 2, chips)),
            dma((2, chips)),
            dma((2, chips)),
            dma((2, chips)),
            dma((2, 2, 2, chips)),
        ],
        compiler_params=pltpu.CompilerParams(
            collective_id=0, has_side_effects=True, vmem_limit_bytes=20 * 2**20
        ),
    )(*inputs)
    return pl.pallas_call(
        finish,
        out_shape=shapes,
        in_specs=[vmem, vmem],
        out_specs=(vmem, vmem),
        compiler_params=pltpu.CompilerParams(vmem_limit_bytes=8 * 2**20),
    )(*outs)


def solution(mesh):
    placed = (P("depth", "tile", None), P("depth", None, None), P("tile", None))
    return jax.shard_map(
        per_device,
        mesh=mesh,
        in_specs=placed,
        out_specs=(P("depth", "tile", None), P("tile", None)),
        check_vma=False,
    )
```

```python
import functools
import math

import jax
import jax.numpy as jnp
import ml_dtypes
import numpy as np
from jax import lax
from jax.experimental import pallas as pl
from jax.experimental.pallas import tpu as pltpu
from jax.sharding import PartitionSpec as P

step_size = 2.0
threshold = 0.5
f32 = jnp.float32
bf16 = jnp.bfloat16
MESH = pl.DeviceIdType.MESH


def halves(table):
    table = table.astype(np.float32)
    high = table.astype(ml_dtypes.bfloat16)
    low = (table - high.astype(np.float32)).astype(ml_dtypes.bfloat16)
    return np.stack([high, low])


def tables(rows, width, size):
    freq_rows, freq_cols = 3 * rows, width + 128
    reach = (size - 1) // 2
    omega = math.pi * (2 * np.arange(freq_cols // 2) + 1) / freq_cols
    across = np.arange(width)[:, None] * omega[None, :]
    col = np.concatenate([np.cos(across), -np.sin(across)], 1)
    back = col.T * (2.0 / (freq_cols * freq_rows))
    across_k = (np.arange(size + 1) - reach)[:, None] * omega[None, :]
    col_k = np.concatenate([np.cos(across_k), -np.sin(across_k)], 1)
    theta = math.pi * (2 * np.arange(freq_rows // 2) + 1) / freq_rows
    place = np.concatenate([np.arange(2 * rows), np.arange(-rows, 0)])
    down = theta[:, None] * place[None, :]
    row = np.concatenate([np.cos(down), np.sin(down)], 0)
    down_k = theta[:, None] * (np.arange(size + 1) - reach)[None, :]
    row_k = np.concatenate([np.cos(down_k), np.sin(down_k)], 0)
    return [halves(t) for t in (col, back, col_k, row, row.T, row_k)]


def split(x):
    high = x.astype(bf16)
    return high, (x - high.astype(f32)).astype(bf16)


def product(a, b):
    left = jnp.concatenate([a[0], a[1], a[0]], axis=1)
    right = jnp.concatenate([b[0], b[0], b[1]], axis=0)
    return jnp.dot(left, right, preferred_element_type=f32)


def spectrum(a):
    m, n = a.shape[0] // 2, a.shape[1] // 2
    cos_real, cos_imaginary, sin_real, sin_imaginary = a[:m, :n], a[:m, n:], a[m:, :n], a[m:, n:]
    return (
        cos_real + sin_imaginary,
        cos_imaginary - sin_real,
        cos_real - sin_imaginary,
        cos_imaginary + sin_real,
    )


def folded(plus_real, plus_imaginary, minus_real, minus_imaginary):
    even = jnp.concatenate([plus_real + minus_real, plus_imaginary + minus_imaginary], axis=1)
    odd = jnp.concatenate([minus_imaginary - plus_imaginary, plus_real - minus_real], axis=1)
    return jnp.concatenate([even, odd], axis=0)


def when(condition, action):
    if condition is None:
        action()
    else:
        pl.when(condition)(action)


def kernel(
    steps,
    nx,
    strips,
    volume_hbm,
    spread_hbm,
    measured_hbm,
    col_hbm,
    back_hbm,
    col_k_hbm,
    row_hbm,
    row_back_hbm,
    row_k_hbm,
    next_ref,
    residual_ref,
    volume_ref,
    spread_ref,
    measured_ref,
    col_ref,
    back_ref,
    col_k_ref,
    row_ref,
    row_back_ref,
    row_k_ref,
    pad_ref,
    optic_ref,
    sum_ref,
    part_ref,
    kept_ref,
    pair_ref,
    held_ref,
    beside_ref,
    own_ref,
    block_ref,
    piece_ref,
    full_ref,
    load_sems,
    pair_sems,
    tile_sems,
    piece_sems,
    final_sems,
    half_sems,
    halo_sems,
):
    depth, tile = lax.axis_index("depth"), lax.axis_index("tile")
    chip, core = depth // 2, depth % 2
    x, y = chip // 2, chip % 2
    partner = chip * 2 + (1 - core)
    above, below = (tile + 1) % strips, (tile + strips - 1) % strips
    has_above, has_below = tile < strips - 1, tile > 0
    chips = len(steps)
    hops = [min(dx, nx - dx) + 2 * dy for dx, dy in steps]
    far = [i for i in range(chips) if hops[i] >= 1]
    far_out = [i for i in range(chips) if hops[i] >= 1]
    targets = [(x + dx) % nx * 2 + (y + dy) % 2 for dx, dy in steps]
    sources = [(x + nx - dx) % nx * 2 + (y + dy) % 2 for dx, dy in steps]
    planes, rows, width = volume_ref.shape
    size = spread_ref.shape[0]
    half_rows = rows // 2
    length = half_rows // chips
    freq_rows, freq_cols = 3 * rows, width + 128
    loads = {}
    order = ("spread", "col_k", "volume", "col", "row_k", "row", "row_back", "back", "measured")
    refs = {
        "spread": (spread_hbm, spread_ref),
        "col_k": (col_k_hbm, col_k_ref),
        "volume": (volume_hbm, volume_ref),
        "col": (col_hbm, col_ref),
        "row_k": (row_k_hbm, row_k_ref),
        "row": (row_hbm, row_ref),
        "row_back": (row_back_hbm, row_back_ref),
        "back": (back_hbm, back_ref),
        "measured": (measured_hbm, measured_ref),
    }
    for i, name in enumerate(order):
        loads[name] = pltpu.make_async_copy(*refs[name], load_sems.at[i])
    for name in order:
        loads[name].start()

    barrier = pltpu.get_barrier_semaphore()
    inside = [partner] + [t * 2 + core for t in targets[1:]]
    across = [depth, partner] + [targets[i] * 2 + core for i in sorted({*far, *far_out})]

    def greet(devices, t):
        for d in devices:
            pl.semaphore_signal(barrier, inc=1, device_id=(d, t), device_id_type=MESH)

    greet(inside, tile)
    when(has_above, lambda: greet(across, above))
    when(has_below, lambda: greet(across, below))
    arrivals = len(inside) + sum(jnp.where(side, len(across), 0) for side in (has_above, has_below))

    sends = []

    def remote(src, dst, sems, index, d, t, going=None, coming=None):
        copy = pltpu.make_async_remote_copy(
            src_ref=src,
            dst_ref=dst,
            send_sem=sems.at[(0, *index)],
            recv_sem=sems.at[(1, *index)],
            device_id=(d, t),
            device_id_type=MESH,
        )
        when(going, copy.start)
        sends.append(lambda: when(going, copy.wait_send))
        return lambda: when(coming, copy.wait_recv)

    sides = ((above, has_above, has_below), (below, has_below, has_above))

    def pair(ref, *index):
        return ref[(0, *index)], ref[(1, *index)]

    pad_ref[...] = jnp.zeros_like(pad_ref)
    loads["spread"].wait()
    for d in range(planes):
        pad_ref[d, 0:size, 0:size] = spread_ref[:, d, :]
    loads["col_k"].wait()
    stacked = pad_ref[...].reshape(planes * (size + 1), size + 1)
    optic_cols = product(split(stacked), pair(col_k_ref))
    loads["volume"].wait()
    loads["col"].wait()
    loads["row_k"].wait()
    loads["row"].wait()
    optic = split(optic_cols[0 * (size + 1) : (0 + 1) * (size + 1)])
    for k, value in enumerate(spectrum(product(pair(row_k_ref), optic))):
        optic_ref[0, k] = value
    plane_cols = product(split(volume_ref[...].reshape(planes * rows, width)), pair(col_ref))
    plane = split(plane_cols[0 * rows : (0 + 1) * rows])
    values = spectrum(product(pair(row_ref, slice(None), slice(0, rows)), plane))
    for k in (0, 2):
        optic_real, optic_imaginary = optic_ref[0, k], optic_ref[0, k + 1]
        real, imaginary = values[k], values[k + 1]
        sum_real = optic_real * real - optic_imaginary * imaginary
        sum_imaginary = optic_real * imaginary + optic_imaginary * real
        sum_ref[k], sum_ref[k + 1] = sum_real, sum_imaginary
    optic = split(optic_cols[1 * (size + 1) : (1 + 1) * (size + 1)])
    for k, value in enumerate(spectrum(product(pair(row_k_ref), optic))):
        optic_ref[1, k] = value
    plane = split(plane_cols[1 * rows : (1 + 1) * rows])
    values = spectrum(product(pair(row_ref, slice(None), slice(0, rows)), plane))
    for k in (0, 2):
        optic_real, optic_imaginary = optic_ref[1, k], optic_ref[1, k + 1]
        real, imaginary = values[k], values[k + 1]
        sum_real = optic_real * real - optic_imaginary * imaginary
        sum_imaginary = optic_real * imaginary + optic_imaginary * real
        sum_ref[k] += sum_real
        sum_ref[k + 1] += sum_imaginary
    total = split(folded(*(sum_ref[k] for k in range(4))))

    def half_of(c):
        first = [pl.multiple_of(b * rows + c * half_rows, half_rows) for b in range(3)]
        part_rows = [jnp.concatenate([row_back_ref[p, pl.ds(f, half_rows), :] for f in first], axis=0) for p in range(2)]
        part = product(split(product(part_rows, total)), pair(back_ref))
        return part.reshape(3, half_rows, width)

    loads["row_back"].wait()
    loads["back"].wait()
    part_ref[...] = half_of(1 - core)
    pl.semaphore_wait(barrier, arrivals)
    paired = {b: remote(part_ref.at[b], pair_ref.at[b], pair_sems, (b,), partner, tile) for b in (1, 2, 0)}
    kept_ref[...] = half_of(core)

    near = {}
    for b in (1, 2):
        paired[b]()
        held_ref[b - 1] = (kept_ref[b] + pair_ref[b]).reshape(chips, length, width)
    for i in reversed(range(chips)):
        for b, side in enumerate(sides):
            to = targets[i] * 2 + core if i in far else depth
            near[b, i] = remote(held_ref.at[b, targets[i]], beside_ref.at[b, i], tile_sems, (b, i), to, *side)
    paired[0]()
    own_ref[...] = (kept_ref[0] + pair_ref[0]).reshape(chips, length, width)

    pieces = {}

    def from_beside(i):
        near[0, i]()
        near[1, i]()
        value = jnp.where(has_below, beside_ref[0, i], 0.0)
        return value + jnp.where(has_above, beside_ref[1, i], 0.0)

    for i in far:
        pieces[i] = remote(own_ref.at[targets[i]], piece_ref.at[i], piece_sems, (i,), targets[i] * 2 + core, tile)
    for i in reversed(range(chips)):
        if i in far:
            continue
        value = own_ref[targets[i]] + from_beside(i)
        if i:
            held_ref[2, i] = value
            pieces[i] = remote(held_ref.at[2, i], piece_ref.at[i], piece_sems, (i,), targets[i] * 2 + core, tile)
    loads["measured"].wait()
    start = pl.multiple_of(core * half_rows + chip * length, length)
    value -= measured_ref[pl.ds(start, length), :]
    for i in range(1, chips):
        pieces[i]()
        value += piece_ref[i]
        if i in far:
            value += from_beside(i)
    full_ref[0, core, chip] = value

    finals, halos, halved = {}, {}, {}
    mine = full_ref.at[0, core, chip]
    for i in reversed(range(1, chips)):
        to = targets[i] * 2 + core
        finals[i] = remote(mine, mine, final_sems, (i,), to, tile)
        if i in far_out:
            for b, side in enumerate(sides):
                halos[b, 0, i] = remote(mine, full_ref.at[2 - b, core, chip], halo_sems, (b, 0, i), to, *side)
    for i in range(chips):
        j = sources[i]
        here = full_ref.at[0, core, j]
        if i:
            finals[i]()
        halved[i] = remote(here, here, half_sems, (i,), partner, tile)
        if i not in far_out:
            for b, side in enumerate(sides):
                for c, d in enumerate((depth, partner)):
                    halos[b, c, i] = remote(here, full_ref.at[2 - b, core, j], halo_sems, (b, c, i), d, *side)
    for i in far_out:
        for b, (_, _, coming) in enumerate(sides):
            halos[b, 0, i]()
            there = full_ref.at[2 - b, core, sources[i]]
            halos[b, 1, i] = remote(there, there, halo_sems, (b, 1, i), partner, tile, coming, coming)
    for i in range(chips):
        halved[i]()

    strip = full_ref[0].reshape(rows, width)
    residual_ref[...] = strip
    strip_cols = split(product(split(strip), pair(col_ref)))
    block_ref[...] = product(pair(row_ref, slice(None), slice(0, rows)), strip_cols)
    for i in range(chips):
        for b in (0, 1):
            for c in (1,) if i in far_out else (0, 1):
                halos[b, c, i]()
    after = jnp.where(has_above, full_ref[1].reshape(rows, width), 0.0)
    before = jnp.where(has_below, full_ref[2].reshape(rows, width), 0.0)
    beside_cols = split(product(split(jnp.concatenate([after, before], axis=0)), pair(col_ref)))
    block_ref[...] += product(pair(row_ref, slice(None), slice(rows, freq_rows)), beside_cols)
    mixed = []
    for d in range(planes):
        values = spectrum(block_ref[...])
        grad = []
        for k in (0, 2):
            optic_real, optic_imaginary = optic_ref[d, k], optic_ref[d, k + 1]
            real, imaginary = values[k], values[k + 1]
            grad.append(optic_real * real + optic_imaginary * imaginary)
            grad.append(optic_real * imaginary - optic_imaginary * real)
        mixed.append(product(pair(row_back_ref, slice(0, rows)), split(folded(*grad))))
    gradient = product(split(jnp.concatenate(mixed, axis=0)), pair(back_ref)).reshape(planes, rows, width)
    shifted = volume_ref[...] - step_size * gradient
    next_ref[...] = shifted - jnp.clip(shifted, -threshold, threshold)
    for wait in sends:
        wait()


def finish(next_ref, residual_ref, next_out, residual_out, sems):
    copies = [
        pltpu.make_async_copy(next_ref, next_out, sems.at[0]),
        pltpu.make_async_copy(residual_ref, residual_out, sems.at[1]),
    ]
    for copy in copies:
        copy.start()
    for copy in copies:
        copy.wait()


def per_device(volume, point_spread, measured):
    planes, rows, width = volume.shape
    size = point_spread.shape[1]
    chips, strips = lax.axis_size("depth") // 2, lax.axis_size("tile")
    nx = chips // 2
    steps = sorted(((dx, dy) for dx in range(nx) for dy in range(2)), key=lambda s: (min(s[0], nx - s[0]) + 2 * s[1], s))
    constants = [jnp.asarray(t) for t in tables(rows, width, size)]
    spread = jnp.transpose(point_spread, (1, 0, 2))
    half_rows = rows // 2
    length = half_rows // chips
    freq_rows, half = 3 * rows, (width + 128) // 2
    vmem = pl.BlockSpec(memory_space=pltpu.VMEM)
    dma = pltpu.SemaphoreType.DMA
    inputs = tuple(pltpu.with_memory_space_constraint(a, pltpu.HBM) for a in (volume, spread, measured, *constants))
    shapes = (jax.ShapeDtypeStruct((planes, rows, width), f32), jax.ShapeDtypeStruct((rows, width), f32))
    outs = pl.pallas_call(
        functools.partial(kernel, steps, nx, strips),
        out_shape=shapes,
        in_specs=[pl.BlockSpec(memory_space=pl.ANY)] * 9,
        out_specs=(vmem, vmem),
        scratch_shapes=[pltpu.VMEM(a.shape, a.dtype) for a in inputs]
        + [
            pltpu.VMEM((planes, size + 1, size + 1), f32),
            pltpu.VMEM((planes, 4, freq_rows // 2, half), f32),
            pltpu.VMEM((4, freq_rows // 2, half), f32),
            pltpu.VMEM((3, half_rows, width), f32),
            pltpu.VMEM((3, half_rows, width), f32),
            pltpu.VMEM((3, half_rows, width), f32),
            pltpu.VMEM((3, chips, length, width), f32),
            pltpu.VMEM((2, chips, length, width), f32),
            pltpu.VMEM((chips, length, width), f32),
            pltpu.VMEM((freq_rows, 2 * half), f32),
            pltpu.VMEM((chips, length, width), f32),
            pltpu.VMEM((3, 2, chips, length, width), f32),
            dma((9,)),
            dma((2, 3)),
            dma((2, 2, chips)),
            dma((2, chips)),
            dma((2, chips)),
            dma((2, chips)),
            dma((2, 2, 2, chips)),
        ],
        compiler_params=pltpu.CompilerParams(
            collective_id=0, has_side_effects=True, vmem_limit_bytes=20 * 2**20
        ),
    )(*inputs)
    return pl.pallas_call(
        finish,
        out_shape=shapes,
        in_specs=[vmem, vmem],
        out_specs=(pl.BlockSpec(memory_space=pl.ANY), pl.BlockSpec(memory_space=pl.ANY)),
        scratch_shapes=[dma((2,))],
        compiler_params=pltpu.CompilerParams(vmem_limit_bytes=8 * 2**20),
    )(*outs)


def solution(mesh):
    placed = (P("depth", "tile", None), P("depth", None, None), P("tile", None))
    return jax.shard_map(
        per_device,
        mesh=mesh,
        in_specs=placed,
        out_specs=(P("depth", "tile", None), P("tile", None)),
        check_vma=False,
    )
```

```python
import functools
import math

import jax
import jax.numpy as jnp
import ml_dtypes
import numpy as np
from jax import lax
from jax.experimental import pallas as pl
from jax.experimental.pallas import tpu as pltpu
from jax.sharding import PartitionSpec as P

step_size = 2.0
threshold = 0.5
f32 = jnp.float32
bf16 = jnp.bfloat16
MESH = pl.DeviceIdType.MESH


def halves(table):
    table = table.astype(np.float32)
    high = table.astype(ml_dtypes.bfloat16)
    low = (table - high.astype(np.float32)).astype(ml_dtypes.bfloat16)
    return np.stack([high, low])


def tables(rows, width, size):
    freq_rows, freq_cols = 3 * rows, width + 128
    reach = (size - 1) // 2
    omega = math.pi * (2 * np.arange(freq_cols // 2) + 1) / freq_cols
    across = np.arange(width)[:, None] * omega[None, :]
    col = np.concatenate([np.cos(across), -np.sin(across)], 1)
    back = col.T * (2.0 / (freq_cols * freq_rows))
    across_k = (np.arange(size + 1) - reach)[:, None] * omega[None, :]
    col_k = np.concatenate([np.cos(across_k), -np.sin(across_k)], 1)
    theta = math.pi * (2 * np.arange(freq_rows // 2) + 1) / freq_rows
    place = np.concatenate([np.arange(2 * rows), np.arange(-rows, 0)])
    down = theta[:, None] * place[None, :]
    row = np.concatenate([np.cos(down), np.sin(down)], 0)
    down_k = theta[:, None] * (np.arange(size + 1) - reach)[None, :]
    row_k = np.concatenate([np.cos(down_k), np.sin(down_k)], 0)
    return [halves(t) for t in (col, back, col_k, row, row.T, row_k)]


def split(x):
    high = x.astype(bf16)
    return high, (x - high.astype(f32)).astype(bf16)


def product(a, b):
    left = jnp.concatenate([a[0], a[1], a[0]], axis=1)
    right = jnp.concatenate([b[0], b[0], b[1]], axis=0)
    return jnp.dot(left, right, preferred_element_type=f32)


def spectrum(a):
    m, n = a.shape[0] // 2, a.shape[1] // 2
    cos_real, cos_imaginary, sin_real, sin_imaginary = a[:m, :n], a[:m, n:], a[m:, :n], a[m:, n:]
    return (
        cos_real + sin_imaginary,
        cos_imaginary - sin_real,
        cos_real - sin_imaginary,
        cos_imaginary + sin_real,
    )


def folded(plus_real, plus_imaginary, minus_real, minus_imaginary):
    even = jnp.concatenate([plus_real + minus_real, plus_imaginary + minus_imaginary], axis=1)
    odd = jnp.concatenate([minus_imaginary - plus_imaginary, plus_real - minus_real], axis=1)
    return jnp.concatenate([even, odd], axis=0)


def when(condition, action):
    if condition is None:
        action()
    else:
        pl.when(condition)(action)


def kernel(
    steps,
    nx,
    strips,
    volume_hbm,
    spread_hbm,
    measured_hbm,
    col_hbm,
    back_hbm,
    col_k_hbm,
    row_hbm,
    row_back_hbm,
    row_k_hbm,
    next_ref,
    residual_ref,
    volume_ref,
    spread_ref,
    measured_ref,
    col_ref,
    back_ref,
    col_k_ref,
    row_ref,
    row_back_ref,
    row_k_ref,
    pad_ref,
    optic_ref,
    sum_ref,
    part_ref,
    kept_ref,
    pair_ref,
    held_ref,
    beside_ref,
    own_ref,
    block_ref,
    piece_ref,
    full_ref,
    load_sems,
    pair_sems,
    tile_sems,
    piece_sems,
    final_sems,
    half_sems,
    halo_sems,
):
    depth, tile = lax.axis_index("depth"), lax.axis_index("tile")
    chip, core = depth // 2, depth % 2
    x, y = chip // 2, chip % 2
    partner = chip * 2 + (1 - core)
    above, below = (tile + 1) % strips, (tile + strips - 1) % strips
    has_above, has_below = tile < strips - 1, tile > 0
    chips = len(steps)
    hops = [min(dx, nx - dx) + 2 * dy for dx, dy in steps]
    far = [i for i in range(chips) if hops[i] >= 1]
    far_out = [i for i in range(chips) if hops[i] >= 1]
    targets = [(x + dx) % nx * 2 + (y + dy) % 2 for dx, dy in steps]
    sources = [(x + nx - dx) % nx * 2 + (y + dy) % 2 for dx, dy in steps]
    planes, rows, width = volume_ref.shape
    size = spread_ref.shape[0]
    half_rows = rows // 2
    length = half_rows // chips
    freq_rows, freq_cols = 3 * rows, width + 128
    loads = {}
    order = ("spread", "col_k", "volume", "col", "row_k", "row", "row_back", "back", "measured")
    refs = {
        "spread": (spread_hbm, spread_ref),
        "col_k": (col_k_hbm, col_k_ref),
        "volume": (volume_hbm, volume_ref),
        "col": (col_hbm, col_ref),
        "row_k": (row_k_hbm, row_k_ref),
        "row": (row_hbm, row_ref),
        "row_back": (row_back_hbm, row_back_ref),
        "back": (back_hbm, back_ref),
        "measured": (measured_hbm, measured_ref),
    }
    for i, name in enumerate(order):
        loads[name] = pltpu.make_async_copy(*refs[name], load_sems.at[i])
    for name in order:
        loads[name].start()

    barrier = pltpu.get_barrier_semaphore()
    inside = [partner] + [t * 2 + core for t in targets[1:]]
    across = [depth, partner] + [targets[i] * 2 + core for i in sorted({*far, *far_out})]

    def greet(devices, t):
        for d in devices:
            pl.semaphore_signal(barrier, inc=1, device_id=(d, t), device_id_type=MESH)

    greet(inside, tile)
    when(has_above, lambda: greet(across, above))
    when(has_below, lambda: greet(across, below))
    arrivals = len(inside) + sum(jnp.where(side, len(across), 0) for side in (has_above, has_below))

    sends = []

    def remote(src, dst, sems, index, d, t, going=None, coming=None):
        copy = pltpu.make_async_remote_copy(
            src_ref=src,
            dst_ref=dst,
            send_sem=sems.at[(0, *index)],
            recv_sem=sems.at[(1, *index)],
            device_id=(d, t),
            device_id_type=MESH,
        )
        when(going, copy.start)
        sends.append(lambda: when(going, copy.wait_send))
        return lambda: when(coming, copy.wait_recv)

    sides = ((above, has_above, has_below), (below, has_below, has_above))

    def pair(ref, *index):
        return ref[(0, *index)], ref[(1, *index)]

    pad_ref[...] = jnp.zeros_like(pad_ref)
    loads["spread"].wait()
    for d in range(planes):
        pad_ref[d, 0:size, 0:size] = spread_ref[:, d, :]
    loads["col_k"].wait()
    stacked = pad_ref[...].reshape(planes * (size + 1), size + 1)
    optic_cols = product(split(stacked), pair(col_k_ref))
    for name in ("volume", "col", "row_k", "row"):
        loads[name].wait()
    half = freq_cols // 2
    chunks = [slice(i * half // 2, (i + 1) * half // 2) for i in range(2)]

    def optic_spectrum(d):
        optic = split(optic_cols[d * (size + 1) : (d + 1) * (size + 1)])
        for k, value in enumerate(spectrum(product(pair(row_k_ref), optic))):
            optic_ref[d, k] = value

    def add_plane(d):
        plane = split(plane_cols[d * rows : (d + 1) * rows])
        for c in chunks:
            beyond = slice(half + c.start, half + c.stop)
            part = [jnp.concatenate([p[:, c], p[:, beyond]], axis=1) for p in plane]
            values = spectrum(product(pair(row_ref, slice(None), slice(0, rows)), part))
            for k in (0, 2):
                optic_real, optic_imaginary = optic_ref[d, k, :, c], optic_ref[d, k + 1, :, c]
                real, imaginary = values[k], values[k + 1]
                sum_real = optic_real * real - optic_imaginary * imaginary
                sum_imaginary = optic_real * imaginary + optic_imaginary * real
                if d == 0:
                    sum_ref[k, :, c], sum_ref[k + 1, :, c] = sum_real, sum_imaginary
                else:
                    sum_ref[k, :, c] += sum_real
                    sum_ref[k + 1, :, c] += sum_imaginary

    optic_spectrum(0)
    plane_cols = product(split(volume_ref[...].reshape(planes * rows, width)), pair(col_ref))
    for d in range(planes):
        if d:
            optic_spectrum(d)
        add_plane(d)
    totals = [split(folded(*(sum_ref[k, :, c] for k in range(4)))) for c in chunks]

    def half_of(c):
        first = [pl.multiple_of(b * rows + c * half_rows, half_rows) for b in range(3)]
        part_rows = [jnp.concatenate([row_back_ref[p, pl.ds(f, half_rows), :] for f in first], axis=0) for p in range(2)]
        mixed = [product(part_rows, total) for total in totals]
        n = mixed[0].shape[1] // 2
        mixed = jnp.concatenate([m[:, :n] for m in mixed] + [m[:, n:] for m in mixed], axis=1)
        part = product(split(mixed), pair(back_ref))
        return part.reshape(3, half_rows, width)

    loads["row_back"].wait()
    loads["back"].wait()
    part_ref[...] = half_of(1 - core)
    pl.semaphore_wait(barrier, arrivals)
    paired = {b: remote(part_ref.at[b], pair_ref.at[b], pair_sems, (b,), partner, tile) for b in (1, 2, 0)}
    kept_ref[...] = half_of(core)

    near = {}
    for b in (1, 2):
        paired[b]()
        held_ref[b - 1] = (kept_ref[b] + pair_ref[b]).reshape(chips, length, width)
    for i in reversed(range(chips)):
        for b, side in enumerate(sides):
            to = targets[i] * 2 + core if i in far else depth
            near[b, i] = remote(held_ref.at[b, targets[i]], beside_ref.at[b, i], tile_sems, (b, i), to, *side)
    paired[0]()
    own_ref[...] = (kept_ref[0] + pair_ref[0]).reshape(chips, length, width)

    pieces = {}

    def from_beside(i):
        near[0, i]()
        near[1, i]()
        value = jnp.where(has_below, beside_ref[0, i], 0.0)
        return value + jnp.where(has_above, beside_ref[1, i], 0.0)

    for i in far:
        pieces[i] = remote(own_ref.at[targets[i]], piece_ref.at[i], piece_sems, (i,), targets[i] * 2 + core, tile)
    for i in reversed(range(chips)):
        if i in far:
            continue
        value = own_ref[targets[i]] + from_beside(i)
        if i:
            held_ref[2, i] = value
            pieces[i] = remote(held_ref.at[2, i], piece_ref.at[i], piece_sems, (i,), targets[i] * 2 + core, tile)
    loads["measured"].wait()
    start = pl.multiple_of(core * half_rows + chip * length, length)
    value -= measured_ref[pl.ds(start, length), :]
    for i in range(1, chips):
        pieces[i]()
        value += piece_ref[i]
        if i in far:
            value += from_beside(i)
    full_ref[0, core, chip] = value

    finals, halos, halved = {}, {}, {}
    mine = full_ref.at[0, core, chip]
    for i in reversed(range(1, chips)):
        to = targets[i] * 2 + core
        finals[i] = remote(mine, mine, final_sems, (i,), to, tile)
        if i in far_out:
            for b, side in enumerate(sides):
                halos[b, 0, i] = remote(mine, full_ref.at[2 - b, core, chip], halo_sems, (b, 0, i), to, *side)
    for i in range(chips):
        j = sources[i]
        here = full_ref.at[0, core, j]
        if i:
            finals[i]()
        halved[i] = remote(here, here, half_sems, (i,), partner, tile)
        if i not in far_out:
            for b, side in enumerate(sides):
                for c, d in enumerate((depth, partner)):
                    halos[b, c, i] = remote(here, full_ref.at[2 - b, core, j], halo_sems, (b, c, i), d, *side)
    for i in far_out:
        for b, (_, _, coming) in enumerate(sides):
            halos[b, 0, i]()
            there = full_ref.at[2 - b, core, sources[i]]
            halos[b, 1, i] = remote(there, there, halo_sems, (b, 1, i), partner, tile, coming, coming)
    for i in range(chips):
        halved[i]()

    strip = full_ref[0].reshape(rows, width)
    residual_ref[...] = strip
    strip_cols = split(product(split(strip), pair(col_ref)))
    block_ref[...] = product(pair(row_ref, slice(None), slice(0, rows)), strip_cols)
    for i in range(chips):
        for b in (0, 1):
            for c in (1,) if i in far_out else (0, 1):
                halos[b, c, i]()
    after = jnp.where(has_above, full_ref[1].reshape(rows, width), 0.0)
    before = jnp.where(has_below, full_ref[2].reshape(rows, width), 0.0)
    beside_cols = split(product(split(jnp.concatenate([after, before], axis=0)), pair(col_ref)))
    block_ref[...] += product(pair(row_ref, slice(None), slice(rows, freq_rows)), beside_cols)
    mixed = []
    for d in range(planes):
        values = spectrum(block_ref[...])
        grad = []
        for k in (0, 2):
            optic_real, optic_imaginary = optic_ref[d, k], optic_ref[d, k + 1]
            real, imaginary = values[k], values[k + 1]
            grad.append(optic_real * real + optic_imaginary * imaginary)
            grad.append(optic_real * imaginary - optic_imaginary * real)
        mixed.append(product(pair(row_back_ref, slice(0, rows)), split(folded(*grad))))
    gradient = product(split(jnp.concatenate(mixed, axis=0)), pair(back_ref)).reshape(planes, rows, width)
    shifted = volume_ref[...] - step_size * gradient
    next_ref[...] = shifted - jnp.clip(shifted, -threshold, threshold)
    for wait in sends:
        wait()


def finish(next_ref, residual_ref, next_out, residual_out, sems):
    copies = [
        pltpu.make_async_copy(next_ref, next_out, sems.at[0]),
        pltpu.make_async_copy(residual_ref, residual_out, sems.at[1]),
    ]
    for copy in copies:
        copy.start()
    for copy in copies:
        copy.wait()


def per_device(volume, point_spread, measured):
    planes, rows, width = volume.shape
    size = point_spread.shape[1]
    chips, strips = lax.axis_size("depth") // 2, lax.axis_size("tile")
    nx = chips // 2
    steps = sorted(((dx, dy) for dx in range(nx) for dy in range(2)), key=lambda s: (min(s[0], nx - s[0]) + 2 * s[1], s))
    constants = [jnp.asarray(t) for t in tables(rows, width, size)]
    spread = jnp.transpose(point_spread, (1, 0, 2))
    half_rows = rows // 2
    length = half_rows // chips
    freq_rows, half = 3 * rows, (width + 128) // 2
    vmem = pl.BlockSpec(memory_space=pltpu.VMEM)
    dma = pltpu.SemaphoreType.DMA
    inputs = tuple(pltpu.with_memory_space_constraint(a, pltpu.HBM) for a in (volume, spread, measured, *constants))
    shapes = (jax.ShapeDtypeStruct((planes, rows, width), f32), jax.ShapeDtypeStruct((rows, width), f32))
    outs = pl.pallas_call(
        functools.partial(kernel, steps, nx, strips),
        out_shape=shapes,
        in_specs=[pl.BlockSpec(memory_space=pl.ANY)] * 9,
        out_specs=(vmem, vmem),
        scratch_shapes=[pltpu.VMEM(a.shape, a.dtype) for a in inputs]
        + [
            pltpu.VMEM((planes, size + 1, size + 1), f32),
            pltpu.VMEM((planes, 4, freq_rows // 2, half), f32),
            pltpu.VMEM((4, freq_rows // 2, half), f32),
            pltpu.VMEM((3, half_rows, width), f32),
            pltpu.VMEM((3, half_rows, width), f32),
            pltpu.VMEM((3, half_rows, width), f32),
            pltpu.VMEM((3, chips, length, width), f32),
            pltpu.VMEM((2, chips, length, width), f32),
            pltpu.VMEM((chips, length, width), f32),
            pltpu.VMEM((freq_rows, 2 * half), f32),
            pltpu.VMEM((chips, length, width), f32),
            pltpu.VMEM((3, 2, chips, length, width), f32),
            dma((9,)),
            dma((2, 3)),
            dma((2, 2, chips)),
            dma((2, chips)),
            dma((2, chips)),
            dma((2, chips)),
            dma((2, 2, 2, chips)),
        ],
        compiler_params=pltpu.CompilerParams(
            collective_id=0, has_side_effects=True, vmem_limit_bytes=20 * 2**20
        ),
    )(*inputs)
    return pl.pallas_call(
        finish,
        out_shape=shapes,
        in_specs=[vmem, vmem],
        out_specs=(pl.BlockSpec(memory_space=pl.ANY), pl.BlockSpec(memory_space=pl.ANY)),
        scratch_shapes=[dma((2,))],
        compiler_params=pltpu.CompilerParams(vmem_limit_bytes=8 * 2**20),
    )(*outs)


def solution(mesh):
    placed = (P("depth", "tile", None), P("depth", None, None), P("tile", None))
    return jax.shard_map(
        per_device,
        mesh=mesh,
        in_specs=placed,
        out_specs=(P("depth", "tile", None), P("tile", None)),
        check_vma=False,
    )
```

```python
import functools
import math

import jax
import jax.numpy as jnp
import ml_dtypes
import numpy as np
from jax import lax
from jax.experimental import pallas as pl
from jax.experimental.pallas import tpu as pltpu
from jax.sharding import PartitionSpec as P

step_size = 2.0
threshold = 0.5
f32 = jnp.float32
bf16 = jnp.bfloat16
MESH = pl.DeviceIdType.MESH


def halves(table):
    table = table.astype(np.float32)
    high = table.astype(ml_dtypes.bfloat16)
    low = (table - high.astype(np.float32)).astype(ml_dtypes.bfloat16)
    return np.stack([high, low])


def tables(rows, width, size):
    freq_rows, freq_cols = 3 * rows, width + 128
    reach = (size - 1) // 2
    omega = math.pi * (2 * np.arange(freq_cols // 2) + 1) / freq_cols
    across = np.arange(width)[:, None] * omega[None, :]
    col = np.concatenate([np.cos(across), -np.sin(across)], 1)
    back = col.T * (2.0 / (freq_cols * freq_rows))
    across_k = (np.arange(size + 1) - reach)[:, None] * omega[None, :]
    col_k = np.concatenate([np.cos(across_k), -np.sin(across_k)], 1)
    theta = math.pi * (2 * np.arange(freq_rows // 2) + 1) / freq_rows
    place = np.concatenate([np.arange(2 * rows), np.arange(-rows, 0)])
    down = theta[:, None] * place[None, :]
    row = np.concatenate([np.cos(down), np.sin(down)], 0)
    down_k = theta[:, None] * (np.arange(size + 1) - reach)[None, :]
    row_k = np.concatenate([np.cos(down_k), np.sin(down_k)], 0)
    return [halves(t) for t in (col, back, col_k, row, row.T, row_k)]


def split(x):
    high = x.astype(bf16)
    return high, (x - high.astype(f32)).astype(bf16)


def product(a, b):
    left = jnp.concatenate([a[0], a[1], a[0]], axis=1)
    right = jnp.concatenate([b[0], b[0], b[1]], axis=0)
    return jnp.dot(left, right, preferred_element_type=f32)


def spectrum(a):
    m, n = a.shape[0] // 2, a.shape[1] // 2
    cos_real, cos_imaginary, sin_real, sin_imaginary = a[:m, :n], a[:m, n:], a[m:, :n], a[m:, n:]
    return (
        cos_real + sin_imaginary,
        cos_imaginary - sin_real,
        cos_real - sin_imaginary,
        cos_imaginary + sin_real,
    )


def folded(plus_real, plus_imaginary, minus_real, minus_imaginary):
    even = jnp.concatenate([plus_real + minus_real, plus_imaginary + minus_imaginary], axis=1)
    odd = jnp.concatenate([minus_imaginary - plus_imaginary, plus_real - minus_real], axis=1)
    return jnp.concatenate([even, odd], axis=0)


def when(condition, action):
    if condition is None:
        action()
    else:
        pl.when(condition)(action)


def kernel(
    steps,
    nx,
    strips,
    volume_hbm,
    spread_hbm,
    measured_hbm,
    col_hbm,
    back_hbm,
    col_k_hbm,
    row_hbm,
    row_back_hbm,
    row_k_hbm,
    next_ref,
    residual_ref,
    volume_ref,
    spread_ref,
    measured_ref,
    col_ref,
    back_ref,
    col_k_ref,
    row_ref,
    row_back_ref,
    row_k_ref,
    pad_ref,
    optic_ref,
    sum_ref,
    part_ref,
    kept_ref,
    pair_ref,
    held_ref,
    beside_ref,
    own_ref,
    block_ref,
    piece_ref,
    full_ref,
    load_sems,
    pair_sems,
    tile_sems,
    piece_sems,
    final_sems,
    half_sems,
    halo_sems,
):
    depth, tile = lax.axis_index("depth"), lax.axis_index("tile")
    chip, core = depth // 2, depth % 2
    x, y = chip // 2, chip % 2
    partner = chip * 2 + (1 - core)
    above, below = (tile + 1) % strips, (tile + strips - 1) % strips
    has_above, has_below = tile < strips - 1, tile > 0
    chips = len(steps)
    hops = [min(dx, nx - dx) + 2 * dy for dx, dy in steps]
    far = [i for i in range(chips) if hops[i] >= 1]
    far_out = [i for i in range(chips) if hops[i] >= 1]
    targets = [(x + dx) % nx * 2 + (y + dy) % 2 for dx, dy in steps]
    sources = [(x + nx - dx) % nx * 2 + (y + dy) % 2 for dx, dy in steps]
    planes, rows, width = volume_ref.shape
    size = spread_ref.shape[0]
    half_rows = rows // 2
    length = half_rows // chips
    freq_rows, freq_cols = 3 * rows, width + 128
    loads = {}
    order = ("spread", "col_k", "volume", "col", "row_k", "row", "row_back", "back", "measured")
    refs = {
        "spread": (spread_hbm, spread_ref),
        "col_k": (col_k_hbm, col_k_ref),
        "volume": (volume_hbm, volume_ref),
        "col": (col_hbm, col_ref),
        "row_k": (row_k_hbm, row_k_ref),
        "row": (row_hbm, row_ref),
        "row_back": (row_back_hbm, row_back_ref),
        "back": (back_hbm, back_ref),
        "measured": (measured_hbm, measured_ref),
    }
    for i, name in enumerate(order):
        loads[name] = pltpu.make_async_copy(*refs[name], load_sems.at[i])
    for name in order:
        loads[name].start()

    barrier = pltpu.get_barrier_semaphore()
    inside = [partner] + [t * 2 + core for t in targets[1:]]
    across = [depth, partner] + [targets[i] * 2 + core for i in sorted({*far, *far_out})]

    def greet(devices, t):
        for d in devices:
            pl.semaphore_signal(barrier, inc=1, device_id=(d, t), device_id_type=MESH)

    greet(inside, tile)
    when(has_above, lambda: greet(across, above))
    when(has_below, lambda: greet(across, below))
    arrivals = len(inside) + sum(jnp.where(side, len(across), 0) for side in (has_above, has_below))

    sends = []

    def remote(src, dst, sems, index, d, t, going=None, coming=None):
        copy = pltpu.make_async_remote_copy(
            src_ref=src,
            dst_ref=dst,
            send_sem=sems.at[(0, *index)],
            recv_sem=sems.at[(1, *index)],
            device_id=(d, t),
            device_id_type=MESH,
        )
        when(going, copy.start)
        sends.append(lambda: when(going, copy.wait_send))
        return lambda: when(coming, copy.wait_recv)

    sides = ((above, has_above, has_below), (below, has_below, has_above))

    def pair(ref, *index):
        return ref[(0, *index)], ref[(1, *index)]

    pad_ref[...] = jnp.zeros_like(pad_ref)
    loads["spread"].wait()
    for d in range(planes):
        pad_ref[d, 0:size, 0:size] = spread_ref[:, d, :]
    loads["col_k"].wait()
    stacked = pad_ref[...].reshape(planes * (size + 1), size + 1)
    optic_cols = product(split(stacked), pair(col_k_ref))
    loads["volume"].wait()
    loads["col"].wait()
    loads["row_k"].wait()
    loads["row"].wait()
    optic = split(optic_cols[0 * (size + 1) : (0 + 1) * (size + 1)])
    for k, value in enumerate(spectrum(product(pair(row_k_ref), optic))):
        optic_ref[0, k] = value
    plane_cols = product(split(volume_ref[...].reshape(planes * rows, width)), pair(col_ref))
    plane = split(plane_cols[0 * rows : (0 + 1) * rows])
    values = spectrum(product(pair(row_ref, slice(None), slice(0, rows)), plane))
    for k in (0, 2):
        optic_real, optic_imaginary = optic_ref[0, k], optic_ref[0, k + 1]
        real, imaginary = values[k], values[k + 1]
        sum_real = optic_real * real - optic_imaginary * imaginary
        sum_imaginary = optic_real * imaginary + optic_imaginary * real
        sum_ref[k], sum_ref[k + 1] = sum_real, sum_imaginary
    optic = split(optic_cols[1 * (size + 1) : (1 + 1) * (size + 1)])
    for k, value in enumerate(spectrum(product(pair(row_k_ref), optic))):
        optic_ref[1, k] = value
    plane = split(plane_cols[1 * rows : (1 + 1) * rows])
    values = spectrum(product(pair(row_ref, slice(None), slice(0, rows)), plane))
    for k in (0, 2):
        optic_real, optic_imaginary = optic_ref[1, k], optic_ref[1, k + 1]
        real, imaginary = values[k], values[k + 1]
        sum_real = optic_real * real - optic_imaginary * imaginary
        sum_imaginary = optic_real * imaginary + optic_imaginary * real
        sum_ref[k] += sum_real
        sum_ref[k + 1] += sum_imaginary
    total = split(folded(*(sum_ref[k] for k in range(4))))

    def half_of(c):
        first = [pl.multiple_of(b * rows + c * half_rows, half_rows) for b in range(3)]
        part_rows = [jnp.concatenate([row_back_ref[p, pl.ds(f, half_rows), :] for f in first], axis=0) for p in range(2)]
        part = product(split(product(part_rows, total)), pair(back_ref))
        return part.reshape(3, half_rows, width)

    loads["row_back"].wait()
    loads["back"].wait()
    part_ref[...] = half_of(1 - core)
    pl.semaphore_wait(barrier, arrivals)
    paired = {b: remote(part_ref.at[b], pair_ref.at[b], pair_sems, (b,), partner, tile) for b in (1, 2, 0)}
    kept_ref[...] = half_of(core)

    near = {}
    for b in (1, 2):
        paired[b]()
        held_ref[b - 1] = (kept_ref[b] + pair_ref[b]).reshape(chips, length, width)
    for i in reversed(range(chips)):
        for b, side in enumerate(sides):
            to = targets[i] * 2 + core if i in far else depth
            near[b, i] = remote(held_ref.at[b, targets[i]], beside_ref.at[b, i], tile_sems, (b, i), to, *side)
    paired[0]()
    own_ref[...] = (kept_ref[0] + pair_ref[0]).reshape(chips, length, width)

    pieces = {}

    def from_beside(i):
        near[0, i]()
        near[1, i]()
        value = jnp.where(has_below, beside_ref[0, i], 0.0)
        return value + jnp.where(has_above, beside_ref[1, i], 0.0)

    for i in far:
        pieces[i] = remote(own_ref.at[targets[i]], piece_ref.at[i], piece_sems, (i,), targets[i] * 2 + core, tile)
    for i in reversed(range(chips)):
        if i in far:
            continue
        value = own_ref[targets[i]] + from_beside(i)
        if i:
            held_ref[2, i] = value
            pieces[i] = remote(held_ref.at[2, i], piece_ref.at[i], piece_sems, (i,), targets[i] * 2 + core, tile)
    loads["measured"].wait()
    start = pl.multiple_of(core * half_rows + chip * length, length)
    value -= measured_ref[pl.ds(start, length), :]
    for i in range(1, chips):
        pieces[i]()
        value += piece_ref[i]
        if i in far:
            value += from_beside(i)
    full_ref[0, core, chip] = value

    finals, halos, halved = {}, {}, {}
    mine = full_ref.at[0, core, chip]
    for i in range(1, chips):
        to = targets[i] * 2 + core
        finals[i] = remote(mine, mine, final_sems, (i,), to, tile)
        if i in far_out:
            for b, side in enumerate(sides):
                halos[b, 0, i] = remote(mine, full_ref.at[2 - b, core, chip], halo_sems, (b, 0, i), to, *side)
    for i in range(chips):
        j = sources[i]
        here = full_ref.at[0, core, j]
        if i:
            finals[i]()
        halved[i] = remote(here, here, half_sems, (i,), partner, tile)
        if i not in far_out:
            for b, side in enumerate(sides):
                for c, d in enumerate((depth, partner)):
                    halos[b, c, i] = remote(here, full_ref.at[2 - b, core, j], halo_sems, (b, c, i), d, *side)
    for i in far_out:
        for b, (_, _, coming) in enumerate(sides):
            halos[b, 0, i]()
            there = full_ref.at[2 - b, core, sources[i]]
            halos[b, 1, i] = remote(there, there, halo_sems, (b, 1, i), partner, tile, coming, coming)
    for i in range(chips):
        halved[i]()

    strip = full_ref[0].reshape(rows, width)
    residual_ref[...] = strip
    strip_cols = split(product(split(strip), pair(col_ref)))
    block_ref[...] = product(pair(row_ref, slice(None), slice(0, rows)), strip_cols)
    for i in range(chips):
        for b in (0, 1):
            for c in (1,) if i in far_out else (0, 1):
                halos[b, c, i]()
    after = jnp.where(has_above, full_ref[1].reshape(rows, width), 0.0)
    before = jnp.where(has_below, full_ref[2].reshape(rows, width), 0.0)
    beside_cols = split(product(split(jnp.concatenate([after, before], axis=0)), pair(col_ref)))
    block_ref[...] += product(pair(row_ref, slice(None), slice(rows, freq_rows)), beside_cols)
    mixed = []
    for d in range(planes):
        values = spectrum(block_ref[...])
        grad = []
        for k in (0, 2):
            optic_real, optic_imaginary = optic_ref[d, k], optic_ref[d, k + 1]
            real, imaginary = values[k], values[k + 1]
            grad.append(optic_real * real + optic_imaginary * imaginary)
            grad.append(optic_real * imaginary - optic_imaginary * real)
        mixed.append(product(pair(row_back_ref, slice(0, rows)), split(folded(*grad))))
    gradient = product(split(jnp.concatenate(mixed, axis=0)), pair(back_ref)).reshape(planes, rows, width)
    shifted = volume_ref[...] - step_size * gradient
    next_ref[...] = shifted - jnp.clip(shifted, -threshold, threshold)
    for wait in sends:
        wait()


def finish(next_ref, residual_ref, next_out, residual_out, sems):
    copies = [
        pltpu.make_async_copy(next_ref, next_out, sems.at[0]),
        pltpu.make_async_copy(residual_ref, residual_out, sems.at[1]),
    ]
    for copy in copies:
        copy.start()
    for copy in copies:
        copy.wait()


def per_device(volume, point_spread, measured):
    planes, rows, width = volume.shape
    size = point_spread.shape[1]
    chips, strips = lax.axis_size("depth") // 2, lax.axis_size("tile")
    nx = chips // 2
    steps = sorted(((dx, dy) for dx in range(nx) for dy in range(2)), key=lambda s: (min(s[0], nx - s[0]) + 2 * s[1], s))
    constants = [jnp.asarray(t) for t in tables(rows, width, size)]
    spread = jnp.transpose(point_spread, (1, 0, 2))
    half_rows = rows // 2
    length = half_rows // chips
    freq_rows, half = 3 * rows, (width + 128) // 2
    vmem = pl.BlockSpec(memory_space=pltpu.VMEM)
    dma = pltpu.SemaphoreType.DMA
    inputs = tuple(pltpu.with_memory_space_constraint(a, pltpu.HBM) for a in (volume, spread, measured, *constants))
    shapes = (jax.ShapeDtypeStruct((planes, rows, width), f32), jax.ShapeDtypeStruct((rows, width), f32))
    outs = pl.pallas_call(
        functools.partial(kernel, steps, nx, strips),
        out_shape=shapes,
        in_specs=[pl.BlockSpec(memory_space=pl.ANY)] * 9,
        out_specs=(vmem, vmem),
        scratch_shapes=[pltpu.VMEM(a.shape, a.dtype) for a in inputs]
        + [
            pltpu.VMEM((planes, size + 1, size + 1), f32),
            pltpu.VMEM((planes, 4, freq_rows // 2, half), f32),
            pltpu.VMEM((4, freq_rows // 2, half), f32),
            pltpu.VMEM((3, half_rows, width), f32),
            pltpu.VMEM((3, half_rows, width), f32),
            pltpu.VMEM((3, half_rows, width), f32),
            pltpu.VMEM((3, chips, length, width), f32),
            pltpu.VMEM((2, chips, length, width), f32),
            pltpu.VMEM((chips, length, width), f32),
            pltpu.VMEM((freq_rows, 2 * half), f32),
            pltpu.VMEM((chips, length, width), f32),
            pltpu.VMEM((3, 2, chips, length, width), f32),
            dma((9,)),
            dma((2, 3)),
            dma((2, 2, chips)),
            dma((2, chips)),
            dma((2, chips)),
            dma((2, chips)),
            dma((2, 2, 2, chips)),
        ],
        compiler_params=pltpu.CompilerParams(
            collective_id=0, has_side_effects=True, vmem_limit_bytes=20 * 2**20
        ),
    )(*inputs)
    return pl.pallas_call(
        finish,
        out_shape=shapes,
        in_specs=[vmem, vmem],
        out_specs=(pl.BlockSpec(memory_space=pl.ANY), pl.BlockSpec(memory_space=pl.ANY)),
        scratch_shapes=[dma((2,))],
        compiler_params=pltpu.CompilerParams(vmem_limit_bytes=8 * 2**20),
    )(*outs)


def solution(mesh):
    placed = (P("depth", "tile", None), P("depth", None, None), P("tile", None))
    return jax.shard_map(
        per_device,
        mesh=mesh,
        in_specs=placed,
        out_specs=(P("depth", "tile", None), P("tile", None)),
        check_vma=False,
    )
```
